32 devices in a mesh: space: 4 (over x, core), dir: 8 (over z, y).
Axes of the slice: x: 2, y: 2, z: 4, core: 2. Of those that a mesh axis runs over, the one named last changes fastest.
Arguments:
- phonon_heat_density: float32 [128, 40, 8, 4, 256], P('dir', None, 'space'), may hold values from 0.01 to 20, as said below
- directions: float32 [3, 128], replicated, may hold values from -1 to 1, as said below
- quad_weight: float32 [128], replicated, may hold values from 0 to 1, as said below
- mirror: int32 [3, 128], replicated, may hold values from 0 to 127, as said below
- band_courant: float32 [40], replicated, may hold values from 0.3 to 1.9
- relax_rate: float32 [40], replicated, may hold values from 0.05 to 0.95
- mode_heat_magnitude: float32 [40], replicated, may hold values from 0.5 to 2
- mode_pulsation: float32 [40], replicated, may hold values from 0.3 to 2.5
- wall_blocks: int32 [4, 16], P('space'), may hold values from 0 to 15, as said below
- wall_count: int32 [4], P('space'), may hold values from 0 to 16, as said below
- wall_facet: int32 [4, 16, 128], P('space'), may hold values from 0 to 6, as said below
Outputs:
- energy_out: float32 [128, 40, 8, 4, 256], P('dir', None, 'space')
- pseudo_kelvin_field: float32 [8, 4, 256], P('space')
The draws below stay inside these ranges and needn't reach their ends.
Inputs may be any that keep to these rules, and one draw needn't show every extreme that they name: Unit vectors with no zero component; negating any one component of a direction gives another of the directions. `quad_weight`: Positive, summing to 1, equal for directions that differ only in the signs of components. mirror[a, d] is the direction whose vector is that of d with component a negated. `phonon_heat_density`: Positive. `wall_blocks`: the entries of each row are distinct blocks of the tile; the first wall_count[t] of them are its wall blocks. `wall_count`: tiles t and t + 2 hold at most 16 wall blocks together; some pair holds exactly that, with one of its tiles at 16. `wall_facet`: 0 marks a cell that is no wall, and every cell of slots from wall_count[t] on; f from 1 to 6 names the facet normal along axis (f - 1) // 2, positive for odd f and negative for even f.
All inputs are finite; a program needn't handle non-finite values.
Results may differ from the reference program's by a relative error of at most 0.0003.
Values sent between devices are 32-bit elements; how exact they have to be, the bound alone decides.
A program may use at most 128 MiB of HBM per device.

```python
import math
import jax
import jax.numpy as jnp
from jax import lax

BANDS = 40
DIRS = 128
NBASE = 16
MESH_DEEP_COUNT = 256
LAYER_HIGH_COUNT = 4
STEPS = 2
NEWTON = 4
BLOCK = 128
WPAIR = 8
WMAX = 16
TILES = 4
MESH_WIDE_COUNT = 8
TILE_BLOCKS = 16


def direction_set(key):
    base_key = jax.random.fold_in(key, 101)
    first_key, second_key, third_key = jax.random.split(base_key, 3)
    cosine = jax.random.uniform(first_key, (NBASE,), jnp.float32, 0.15, 0.95)
    azimuth = jax.random.uniform(second_key, (NBASE,), jnp.float32, 0.15, 1.42)
    radial = jnp.sqrt(1.0 - cosine * cosine)
    base_vectors = jnp.stack([radial * jnp.cos(azimuth), radial * jnp.sin(azimuth), cosine])
    base_weight = jnp.exp(jax.random.uniform(third_key, (NBASE,), jnp.float32, jnp.log(0.3), jnp.log(3.0)))
    ordering = jax.random.permutation(jax.random.fold_in(key, 102), DIRS).astype(jnp.int32)
    octant = ordering // NBASE
    member = ordering % NBASE
    return (base_vectors, base_weight, ordering, octant, member)


def octant_bit(octant, axis_num):
    return octant // 2 ** axis_num % 2


def draw_directions(key, part):
    base_vectors, base_weight, ordering, octant, member = direction_set(key)
    rows = []
    for axis_num in range(3):
        signs = (1 - 2 * octant_bit(octant, axis_num)).astype(jnp.float32)
        rows.append(signs * base_vectors[axis_num][member])
    return jnp.stack(rows).astype(jnp.float32)


def draw_quad_weight(key, part):
    base_vectors, base_weight, ordering, octant, member = direction_set(key)
    return (base_weight[member] / (8.0 * jnp.sum(base_weight))).astype(jnp.float32)


def draw_mirror(key, part):
    base_vectors, base_weight, ordering, octant, member = direction_set(key)
    inverse = jnp.argsort(ordering).astype(jnp.int32)
    rows = []
    for axis_num in range(3):
        flipped = octant + (1 - 2 * octant_bit(octant, axis_num)) * 2 ** axis_num
        rows.append(inverse[flipped * NBASE + member])
    return jnp.stack(rows).astype(jnp.int32)


def draw_phonon_heat_density(key, part):
    cell_key, entry_key = jax.random.split(jax.random.fold_in(key, 1), 2)
    full_shape = (DIRS, BANDS, MESH_WIDE_COUNT, LAYER_HIGH_COUNT, MESH_DEEP_COUNT)
    scale = jnp.exp(jax.random.uniform(cell_key, (MESH_WIDE_COUNT, LAYER_HIGH_COUNT, MESH_DEEP_COUNT), jnp.float32, jnp.log(0.2), jnp.log(5.0)))
    factor = jnp.exp(jax.random.uniform(entry_key, full_shape, jnp.float32, jnp.log(0.2), jnp.log(2.0)))
    return (factor * scale[None, None]).astype(jnp.float32)


def wall_layout(key):
    layout_key = jax.random.fold_in(key, 201)
    block_key, count_key, facet_key = jax.random.split(layout_key, 3)
    tile_keys = jax.random.split(block_key, TILES)

    def pick_blocks(one_key):
        return jax.random.permutation(one_key, TILE_BLOCKS)[:WMAX]
    blocks = jax.vmap(pick_blocks)(tile_keys).astype(jnp.int32)
    half_tiles = TILES // 2
    large_key, small_key, force_key, flip_key = jax.random.split(count_key, 4)
    larger = jax.random.randint(large_key, (half_tiles,), WPAIR, WMAX + 1)
    forced = jax.random.randint(force_key, (), 0, half_tiles)
    larger = jnp.where(jnp.arange(half_tiles) == forced, WMAX, larger)
    smaller = jax.random.randint(small_key, (half_tiles,), 0, WMAX - larger + 1)
    flips = jax.random.randint(flip_key, (half_tiles,), 0, 2)
    first_half = jnp.where(flips == 1, larger, smaller)
    second_half = jnp.where(flips == 1, smaller, larger)
    counts = jnp.concatenate([first_half, second_half]).astype(jnp.int32)
    facets = jax.random.randint(facet_key, (TILES, WMAX, BLOCK), 0, 7)
    slot_ids = jnp.arange(WMAX, dtype=jnp.int32)
    facets = jnp.where(slot_ids[None, :, None] < counts[:, None, None], facets, 0).astype(jnp.int32)
    return (blocks, counts, facets)


def draw_wall_blocks(key, part):
    return wall_layout(key)[0]


def draw_wall_count(key, part):
    return wall_layout(key)[1]


def draw_wall_facet(key, part):
    return wall_layout(key)[2]


def setup_inputs(seed: int = 0) -> dict:
    arg_keys = jax.random.split(jax.random.key(seed), 12)
    return {
        "phonon_heat_density": draw_phonon_heat_density(jax.random.fold_in(arg_keys[11], 71), 0),
        "directions": draw_directions(jax.random.fold_in(arg_keys[11], 71), 0),
        "quad_weight": draw_quad_weight(jax.random.fold_in(arg_keys[11], 71), 0),
        "mirror": draw_mirror(jax.random.fold_in(arg_keys[11], 71), 0),
        "band_courant": jnp.clip(jax.random.uniform(arg_keys[4], (BANDS,), jnp.float32, 0.3, 1.9), 0.3, 1.9),
        "relax_rate": jnp.clip(jnp.exp(jax.random.uniform(arg_keys[5], (BANDS,), jnp.float32, math.log(0.05), math.log(0.95))), 0.05, 0.95),
        "mode_heat_magnitude": jnp.clip(jnp.exp(jax.random.uniform(arg_keys[6], (BANDS,), jnp.float32, math.log(0.5), math.log(2.0))), 0.5, 2.0),
        "mode_pulsation": jnp.clip(jnp.exp(jax.random.uniform(arg_keys[7], (BANDS,), jnp.float32, math.log(0.3), math.log(2.5))), 0.3, 2.5),
        "wall_blocks": draw_wall_blocks(jax.random.fold_in(arg_keys[11], 71), 0),
        "wall_count": draw_wall_count(jax.random.fold_in(arg_keys[11], 71), 0),
        "wall_facet": draw_wall_facet(jax.random.fold_in(arg_keys[11], 71), 0),
    }


def beam_coeffs(courant):
    abs_speed = jnp.abs(courant)
    centre = 1.0 - 1.5 * abs_speed + 0.5 * abs_speed * abs_speed
    near_weight = 2.0 * abs_speed - abs_speed * abs_speed
    far_weight = 0.5 * abs_speed * abs_speed - 0.5 * abs_speed
    forward = courant > 0
    return (centre, jnp.where(forward, near_weight, 0.0), jnp.where(forward, far_weight, 0.0),
            jnp.where(forward, 0.0, near_weight), jnp.where(forward, 0.0, far_weight))


def combine(coeffs, centre_field, back_one, back_two, fore_one, fore_two):
    return (coeffs[0] * centre_field + coeffs[1] * back_one + coeffs[2] * back_two
            + coeffs[3] * fore_one + coeffs[4] * fore_two)


def roll_sweep(field_in, coeffs, axis_num):
    return combine(coeffs, field_in, jnp.roll(field_in, 1, axis_num), jnp.roll(field_in, 2, axis_num),
                   jnp.roll(field_in, -1, axis_num), jnp.roll(field_in, -2, axis_num))


def root_finder_guess(injection_contribution, collision_speed_factor, mode_pulsation):
    pseudo_kelvin_field = jnp.ones_like(injection_contribution)
    for newton_turn in range(NEWTON):
        dimensionless_pulsation = mode_pulsation[:, None] / pseudo_kelvin_field[None, :]
        heat_surplus = jnp.expm1(dimensionless_pulsation)
        mismatch_error = jnp.sum(collision_speed_factor[:, None] / heat_surplus, axis=0) - injection_contribution
        gradient_guess = jnp.sum(collision_speed_factor[:, None] * dimensionless_pulsation * jnp.exp(dimensionless_pulsation) / (heat_surplus * heat_surplus), axis=0) / pseudo_kelvin_field
        pseudo_kelvin_field = jnp.clip(pseudo_kelvin_field - mismatch_error / gradient_guess, 0.5 * pseudo_kelvin_field, 2.0 * pseudo_kelvin_field)
    return pseudo_kelvin_field


def reflect_walls(phonon_heat_density, directions, mirror, wall_blocks, wall_count, wall_facet):
    grid_view = phonon_heat_density.reshape(DIRS, BANDS, TILES, TILE_BLOCKS, BLOCK)
    tile_ids = jnp.arange(TILES, dtype=jnp.int32)[:, None]
    walls = grid_view[:, :, tile_ids, wall_blocks]
    slot_ids = jnp.arange(WMAX, dtype=jnp.int32)
    facets = jnp.where(slot_ids[None, :, None] < wall_count[:, None, None], wall_facet, 0)
    result = walls
    for axis_num in range(3):
        mirrored = walls[mirror[axis_num]]
        component = directions[axis_num][:, None, None, None, None]
        chosen = (((facets == 2 * axis_num + 1)[None, None] & (component > 0))
                  | ((facets == 2 * axis_num + 2)[None, None] & (component < 0)))
        result = jnp.where(chosen, mirrored, result)
    grid_view = grid_view.at[:, :, tile_ids, wall_blocks].set(result)
    return grid_view.reshape(phonon_heat_density.shape)


def reference(phonon_heat_density, directions, quad_weight, mirror, band_courant, relax_rate, mode_heat_magnitude, mode_pulsation, wall_blocks, wall_count, wall_facet):
    def move_one(pair):
        field_in, unit_vec = pair
        moved = roll_sweep(field_in, beam_coeffs((unit_vec[0] * band_courant)[:, None, None, None]), 1)
        moved = roll_sweep(moved, beam_coeffs((unit_vec[1] * band_courant)[:, None, None, None]), 3)
        moved = roll_sweep(moved, beam_coeffs((unit_vec[2] * band_courant)[:, None, None, None]), 2)
        return moved

    weights = (quad_weight[:, None] * relax_rate[None, :]).reshape(-1)
    collision_speed_factor = relax_rate * mode_heat_magnitude
    pseudo_kelvin_field = jnp.ones((MESH_WIDE_COUNT * LAYER_HIGH_COUNT * MESH_DEEP_COUNT,), jnp.float32)
    for step_num in range(STEPS):
        phonon_heat_density = reflect_walls(phonon_heat_density, directions, mirror, wall_blocks, wall_count, wall_facet)
        phonon_heat_density = lax.map(move_one, (phonon_heat_density, directions.T))
        injection_contribution = jnp.tensordot(weights, phonon_heat_density.reshape(DIRS * BANDS, MESH_WIDE_COUNT * LAYER_HIGH_COUNT * MESH_DEEP_COUNT), axes=1, precision=lax.Precision.HIGHEST)
        pseudo_kelvin_field = root_finder_guess(injection_contribution, collision_speed_factor, mode_pulsation)
        bose_einstein_heat = mode_heat_magnitude[:, None] / jnp.expm1(mode_pulsation[:, None] / pseudo_kelvin_field[None, :])
        phonon_heat_density = phonon_heat_density + relax_rate[None, :, None, None, None] * (bose_einstein_heat.reshape(1, BANDS, MESH_WIDE_COUNT, LAYER_HIGH_COUNT, MESH_DEEP_COUNT) - phonon_heat_density)
    return phonon_heat_density, pseudo_kelvin_field.reshape(MESH_WIDE_COUNT, LAYER_HIGH_COUNT, MESH_DEEP_COUNT)
```

```python
import functools

import jax
import jax.numpy as jnp
from jax import lax
from jax.experimental import pallas as pl
from jax.experimental.pallas import tpu as pltpu
from jax.sharding import PartitionSpec as P

NEWTON = 4
BLOCK = 128
OCT = 8


def pick(values, index):
    hits = index[:, None] == jnp.arange(values.shape[0], dtype=jnp.int32)[None, :]
    return jnp.sum(jnp.where(hits, values[None, :], jnp.zeros((), values.dtype)), axis=1)


def orbit_order(directions, mirror):
    count = directions.shape[1]
    ids = jnp.arange(count, dtype=jnp.int32)
    positive = (directions > 0).astype(jnp.int32)
    code = positive[0] + 2 * positive[1] + 4 * positive[2]
    rep = ids
    for axis_num in range(3):
        flipped = pick(mirror[axis_num], rep)
        rep = jnp.where(positive[axis_num] > 0, rep, flipped)
    is_rep = code == 7
    rank_of_rep = jnp.sum(
        jnp.where(is_rep[None, :] & (ids[None, :] < rep[:, None]), 1, 0), axis=1
    ).astype(jnp.int32)
    position = rank_of_rep * OCT + code
    order = jnp.sum(
        jnp.where(position[None, :] == ids[:, None], ids[None, :], 0), axis=1
    ).astype(jnp.int32)
    return order, position


def facet_grid(wall_blocks, wall_count, wall_facet, tile_blocks):
    slot_ids = jnp.arange(wall_blocks.shape[0], dtype=jnp.int32)
    hits = (wall_blocks[None, :] == jnp.arange(tile_blocks, dtype=jnp.int32)[:, None]) & (
        slot_ids < wall_count
    )[None, :]
    return jnp.sum(jnp.where(hits[:, :, None], wall_facet[None], 0), axis=1).astype(jnp.int32)


def roll(u, by, axis):
    return pltpu.roll(u, by % u.shape[axis], axis)


def unit_coeffs(scalars, band, orbit):
    order_ref, directions_ref, weight_ref, courant_ref, rate_ref = scalars
    bands = courant_ref.shape[0]
    real = band < bands
    index = jnp.minimum(band, bands - 1)
    courant, rate = courant_ref[index], jnp.where(real, rate_ref[index], 0.0)
    rep = order_ref[orbit * OCT + OCT - 1]
    coef = []
    for axis_num in range(3):
        coef.extend(beam_coeffs(courant * jnp.abs(directions_ref[axis_num, rep])))
    coef.append(rate * weight_ref[rep])
    return coef, rate


def surplus_of(q):
    series = jnp.ones_like(q)
    for n in range(9, 1, -1):
        series = 1.0 + series * (q * (1.0 / n))
    return jnp.where(q < 0.5, q * series, jnp.exp(q) - 1.0)


def newton(rate_ref, magnitude_ref, pulsation_ref, source):
    kelvin = jnp.ones_like(source)
    for newton_turn in range(NEWTON):
        inverse = 1.0 / kelvin

        def one(b, carry):
            mismatch, gradient = carry
            factor = rate_ref[b] * magnitude_ref[b]
            q = pulsation_ref[b] * inverse
            surplus = surplus_of(q)
            ratio = 1.0 / surplus
            term = factor * ratio
            return mismatch + term, gradient + term * q * ((surplus + 1.0) * ratio)

        zero = jnp.zeros_like(source)
        mismatch, gradient = lax.fori_loop(0, rate_ref.shape[0], one, (zero, zero), unroll=8)
        mismatch, gradient = mismatch - source, gradient * inverse
        kelvin = jnp.clip(kelvin - mismatch / gradient, 0.5 * kelvin, 2.0 * kelvin)
    return kelvin


def sweep_unit(high, tiles, coef, facets_ref, load, store):
    _, rows, width = facets_ref.shape
    row_id = lax.broadcasted_iota(jnp.int32, (rows, width), 0)
    height = row_id % high
    total = [jnp.zeros((rows, width), jnp.float32) for _ in range(tiles)]
    for o in range(OCT):
        way = [1 if o >> a & 1 else -1 for a in range(3)]
        cells = []
        for t in range(tiles):
            facets = facets_ref[t]
            u = load(t, o)
            for a in range(3):
                facing = float(2 * a + 1 if way[a] > 0 else 2 * a + 2)
                u = jnp.where(facets == facing, load(t, o ^ (1 << a)), u)
            cells.append(u)
        turned = [roll(u, high * way[0], 0) for u in cells]
        for t in range(tiles):
            up = (t - way[0]) % tiles
            edge = row_id < high if way[0] > 0 else row_id >= rows - high
            near = jnp.where(edge, turned[up], turned[t])
            u = coef[0] * cells[t] + coef[1] * near + coef[2] * cells[up]
            u = coef[3] * u + coef[4] * roll(u, way[1], 1) + coef[5] * roll(u, 2 * way[1], 1)
            wrap1 = height < 1 if way[2] > 0 else height >= high - 1
            wrap2 = height < 2 if way[2] > 0 else height >= high - 2
            near = jnp.where(wrap1, roll(u, (1 - high) * way[2], 0), roll(u, way[2], 0))
            far = jnp.where(wrap2, roll(u, (2 - high) * way[2], 0), roll(u, 2 * way[2], 0))
            u = coef[6] * u + coef[7] * near + coef[8] * far
            store(t, o, u)
            total[t] = total[t] + u
    return [coef[9] * total[t] for t in range(tiles)]


MESH = pl.DeviceIdType.MESH


def greet(tile, tiles, group, groups):
    barrier = pltpu.get_barrier_semaphore()
    for u in range(1, tiles):
        pl.semaphore_signal(
            barrier, inc=1, device_id=(lax.rem(tile + u, tiles), group), device_id_type=MESH
        )
    for t in range(1, groups):
        pl.semaphore_signal(
            barrier, inc=1, device_id=(tile, lax.rem(group + t, groups)), device_id_type=MESH
        )
    pl.semaphore_wait(barrier, tiles + groups - 2)


def remote(src, dst, send, recv, device):
    return pltpu.make_async_remote_copy(
        src_ref=src, dst_ref=dst, send_sem=send, recv_sem=recv, device_id=device, device_id_type=MESH
    )


def steps_kernel(
    tiles, groups, position_ref, order_ref, directions_ref, weight_ref, courant_ref, rate_ref,
    magnitude_ref, pulsation_ref, facet_ref, home_ref, out_ref, kelvin_ref, *scratch
):
    scalars = (order_ref, directions_ref, weight_ref, courant_ref, rate_ref)
    local_dirs, slots, wide, high, deep = home_ref.shape
    share, rows, bands = slots // groups, wide * high, courant_ref.shape[0]
    dirs = local_dirs * groups
    part = dirs // tiles
    orbits = part // OCT
    landed, sorted_refs, fields, swept, back, unsorted = (
        scratch[n * share : (n + 1) * share] for n in range(6)
    )
    (
        home_back, between, facets_ref, source_ref, near, summed, far, found, kelvins,
        dir_send, dir_recv, tile_send, tile_recv, rev_send, rev_recv, ret_send, ret_recv,
        facet_send, facet_recv, near_send, near_recv, far_send, far_recv, last_send, last_recv, own_sem,
    ) = scratch[6 * share :]
    tile, group = lax.axis_index("space"), lax.axis_index("dir")

    def to_tiles(u):
        return (lax.rem(tile + u, tiles), group)

    def to_groups(t):
        return (tile, lax.rem(group + t, groups))

    own = [
        pltpu.make_async_copy(
            home_ref.at[:, group * share + k],
            landed[k].at[pl.ds(group * local_dirs, local_dirs)],
            own_sem.at[0, k],
        )
        for k in range(share)
    ]
    for copy in own:
        copy.start()
    own_facets = pltpu.make_async_copy(facet_ref, facets_ref.at[tile], own_sem.at[4, 0])
    own_facets.start()
    greet(tile, tiles, group, groups)

    first = []
    for k in range(share):
        line = []
        for t in range(1, groups):
            peer = lax.rem(group + t, groups)
            copy = remote(
                home_ref.at[:, peer * share + k],
                landed[k].at[pl.ds(group * local_dirs, local_dirs)],
                dir_send.at[k, t],
                dir_recv.at[k, t],
                to_groups(t),
            )
            copy.start()
            line.append(copy)
        first.append(line)
    third = []
    for u in range(1, tiles):
        copy = remote(
            facet_ref, facets_ref.at[tile], facet_send.at[u], facet_recv.at[u], to_tiles(u)
        )
        copy.start()
        third.append(copy)
    source_ref[...] = jnp.zeros_like(source_ref)

    second, fourth, fifth = [], [], []

    def gather(k):
        own[k].wait()
        for copy in first[k]:
            copy.wait_recv()

        def move(j, carry):
            d = order_ref[j]
            for x in range(wide):
                sorted_refs[k][j, x * high : (x + 1) * high, :] = landed[k][d, x]
            return carry

        lax.fori_loop(0, dirs, move, 0, unroll=4)
        line = [
            pltpu.make_async_copy(
                sorted_refs[k].at[pl.ds(tile * part, part)], fields[k].at[tile], own_sem.at[1, k]
            )
        ]
        for u in range(1, tiles):
            peer = lax.rem(tile + u, tiles)
            line.append(
                remote(
                    sorted_refs[k].at[pl.ds(peer * part, part)],
                    fields[k].at[tile],
                    tile_send.at[k, u],
                    tile_recv.at[k, u],
                    to_tiles(u),
                )
            )
        for copy in line:
            copy.start()
        second.append(line)

    def sweep(k):
        second[k][0].wait()
        for copy in second[k][1:]:
            copy.wait_recv()

        def one(orbit, carry):
            coef, rate = unit_coeffs(scalars, group * share + k, tile * orbits + orbit)

            def keep_between(t, o, u):
                between[t, o] = u

            sums = sweep_unit(
                high, tiles, coef, facets_ref, lambda t, o: fields[k][t, orbit * OCT + o], keep_between
            )
            for t in range(tiles):
                source_ref[0, t] = source_ref[0, t] + sums[t]
            left = 1.0 - rate
            coef = coef[:6] + [left * c for c in coef[6:9]] + coef[9:]

            def keep_swept(t, o, u):
                swept[k][t, orbit * OCT + o] = left * u

            sums = sweep_unit(
                high, tiles, coef, facets_ref, lambda t, o: between[t, o], keep_swept
            )
            for t in range(tiles):
                source_ref[1, t] = source_ref[1, t] + sums[t]
            return carry

        lax.fori_loop(0, orbits, one, 0)

    def turn(k):
        line = [
            pltpu.make_async_copy(
                swept[k].at[tile], back[k].at[pl.ds(tile * part, part)], own_sem.at[2, k]
            )
        ]
        for u in range(1, tiles):
            peer = lax.rem(tile + u, tiles)
            line.append(
                remote(
                    swept[k].at[peer],
                    back[k].at[pl.ds(tile * part, part)],
                    rev_send.at[k, u],
                    rev_recv.at[k, u],
                    to_tiles(u),
                )
            )
        for copy in line:
            copy.start()
        fourth.append(line)

    def scatter(k):
        fourth[k][0].wait()
        for copy in fourth[k][1:]:
            copy.wait_recv()

        def move(d, carry):
            j = position_ref[d]
            for x in range(wide):
                unsorted[k][d, x] = back[k][j, x * high : (x + 1) * high, :]
            return carry

        lax.fori_loop(0, dirs, move, 0, unroll=4)

    def send_home(k):
        line = [
            pltpu.make_async_copy(
                unsorted[k].at[pl.ds(group * local_dirs, local_dirs)],
                home_back.at[:, group * share + k],
                own_sem.at[3, k],
            )
        ]
        for t in range(1, groups):
            peer = lax.rem(group + t, groups)
            line.append(
                remote(
                    unsorted[k].at[pl.ds(peer * local_dirs, local_dirs)],
                    home_back.at[:, group * share + k],
                    ret_send.at[k, t],
                    ret_recv.at[k, t],
                    to_groups(t),
                )
            )
        for copy in line:
            copy.start()
        fifth.append(line)

    def sum_groups(n):
        copies = []
        for t in range(1, groups):
            copy = remote(
                summed.at[n], far.at[n, group], far_send.at[n, t], far_recv.at[n, t], to_groups(t)
            )
            copy.start()
            copies.append(copy)
        far[n, group] = summed[n]
        return copies

    def total_of(n, copies):
        for copy in copies:
            copy.wait_recv()
        value = far[n, 0]
        for g in range(1, groups):
            value = value + far[n, g]
        return newton(rate_ref, magnitude_ref, pulsation_ref, value)

    for k in range(share):
        gather(k)
        if k == 0:
            own_facets.wait()
            for copy in third:
                copy.wait_recv()
        if k > 0:
            if k + 1 < share or share < 3:
                sweep(k - 1)
                turn(k - 1)
        if k + 2 < share and k > 1:
            scatter(k - 2)
            send_home(k - 2)
        if k + 2 == share and share > 2:
            sweep(k)
            turn(k)
            if k > 1:
                scatter(k - 2)
                send_home(k - 2)
    last = share - 1
    sweep(last)

    nears = []
    for u in range(1, tiles):
        peer = lax.rem(tile + u, tiles)
        copy = remote(
            source_ref.at[:, peer], near.at[u], near_send.at[u], near_recv.at[u], to_tiles(u)
        )
        copy.start()
        nears.append(copy)
    turn(last)
    value = source_ref[:, tile]
    for u in range(1, tiles):
        nears[u - 1].wait_recv()
        value = value + near[u]
    summed[...] = value
    fars = sum_groups(0)
    while len(fifth) < share - 1:
        scatter(len(fifth))
        send_home(len(fifth))
    value = total_of(0, fars)
    found[...] = value
    lasts = []
    for u in range(1, tiles):
        copy = remote(
            found, kelvins.at[tile], last_send.at[u], last_recv.at[u], to_tiles(u)
        )
        copy.start()
        lasts.append(copy)
    kelvins[tile] = value
    for copy in lasts:
        copy.wait_recv()

    below, above = lax.rem(tile + tiles - 1, tiles), lax.rem(tile + 1, tiles)
    row_id = lax.broadcasted_iota(jnp.int32, (rows, deep), 0)
    height = row_id % high

    def drift(b, acc):
        rate, courant = rate_ref[b], courant_ref[b]

        def bose(t):
            return magnitude_ref[b] / surplus_of(pulsation_ref[b] / kelvins[t])

        mine, low, up = bose(tile), bose(below), bose(above)
        shifted = [
            mine,
            jnp.where(row_id < high, roll(low, high, 0), roll(mine, high, 0)),
            low,
            jnp.where(row_id >= rows - high, roll(up, -high, 0), roll(mine, -high, 0)),
            up,
        ]

        def one(d, acc):
            index = group * local_dirs + d
            coef = [both_ways(courant * directions_ref[a, index]) for a in range(3)]
            u = combine(coef[0], shifted)
            u = combine(coef[1], [u] + [roll(u, n, 1) for n in (1, 2, -1, -2)])
            moves = [u]
            for n in (1, 2, -1, -2):
                wrap = height < n if n > 0 else height >= high + n
                whole = high if n > 0 else -high
                moves.append(jnp.where(wrap, roll(u, n - whole, 0), roll(u, n, 0)))
            u = combine(coef[2], moves)
            kept = ((1.0 - rate) * rate) * u
            for x in range(wide):
                out_ref[d, b, x] = kept[x * high : (x + 1) * high]
            return acc + (rate * rate * weight_ref[index]) * u

        return lax.fori_loop(0, local_dirs, one, acc, unroll=2)

    acc = lax.fori_loop(0, bands, drift, jnp.zeros((rows, deep), jnp.float32))
    summed[1] = summed[1] + acc
    fars = fars + sum_groups(1)
    scatter(last)
    send_home(last)
    value = total_of(1, fars[groups - 1 :])
    kelvin_ref[...] = value

    def settle(b, carry):
        heat = rate_ref[b] * (magnitude_ref[b] / surplus_of(pulsation_ref[b] / kelvin_ref[...]))

        def one(d, carry):
            for x in range(wide):
                out_ref[d, b, x] = out_ref[d, b, x] + heat[x * high : (x + 1) * high]
            return carry

        return lax.fori_loop(0, local_dirs, one, carry, unroll=4)

    lax.fori_loop(0, bands, settle, 0)
    for k in range(share):
        fifth[k][0].wait()
        for copy in fifth[k][1:]:
            copy.wait_recv()

        def one(d, carry):
            for g in range(groups):
                b = g * share + k
                if b < bands:
                    for x in range(wide):
                        out_ref[d, b, x] = out_ref[d, b, x] + home_back[d, b, x]
            return carry

        lax.fori_loop(0, local_dirs, one, 0, unroll=2)
    for copy in third + nears + fars + lasts:
        copy.wait_send()
    for line in first:
        for copy in line:
            copy.wait_send()
    for line in second + fourth + fifth:
        for copy in line[1:]:
            copy.wait_send()


def both_ways(speed):
    centre, near, far = beam_coeffs(jnp.abs(speed))
    forward = speed > 0
    return (
        centre,
        jnp.where(forward, near, 0.0),
        jnp.where(forward, far, 0.0),
        jnp.where(forward, 0.0, near),
        jnp.where(forward, 0.0, far),
    )


def combine(coef, moves):
    total = coef[0] * moves[0]
    for c, move in zip(coef[1:], moves[1:]):
        total = total + c * move
    return total


def steps(tiles, groups, share, position, scalars, facets, home):
    local_dirs, _, wide, high, deep = home.shape
    dirs, rows = local_dirs * groups, wide * high
    part = dirs // tiles
    bands = scalars[3].shape[0]
    vmem = pl.BlockSpec(memory_space=pltpu.VMEM)
    smem = pl.BlockSpec(memory_space=pltpu.SMEM)
    anywhere = pl.BlockSpec(memory_space=pl.ANY)
    dma = pltpu.SemaphoreType.DMA
    scratch = (
        [pltpu.VMEM((dirs, wide, high, deep), jnp.float32)] * share
        + [pltpu.VMEM((dirs, rows, deep), jnp.float32)] * share
        + [pltpu.VMEM((tiles, part, rows, deep), jnp.float32)] * (2 * share)
        + [pltpu.VMEM((dirs, rows, deep), jnp.float32)] * share
        + [pltpu.VMEM((dirs, wide, high, deep), jnp.float32)] * share
        + [
            pltpu.VMEM((local_dirs, share * groups, wide, high, deep), jnp.float32),
            pltpu.VMEM((tiles, OCT, rows, deep), jnp.float32),
            pltpu.VMEM((tiles, rows, deep), jnp.float32),
            pltpu.VMEM((2, tiles, rows, deep), jnp.float32),
            pltpu.VMEM((tiles, 2, rows, deep), jnp.float32),
            pltpu.VMEM((2, rows, deep), jnp.float32),
            pltpu.VMEM((2, groups, rows, deep), jnp.float32),
            pltpu.VMEM((rows, deep), jnp.float32),
            pltpu.VMEM((tiles, rows, deep), jnp.float32),
            dma((share, groups)),
            dma((share, groups)),
            dma((share, tiles)),
            dma((share, tiles)),
            dma((share, tiles)),
            dma((share, tiles)),
            dma((share, groups)),
            dma((share, groups)),
            dma((tiles,)),
            dma((tiles,)),
            dma((tiles,)),
            dma((tiles,)),
            dma((2, groups)),
            dma((2, groups)),
            dma((tiles,)),
            dma((tiles,)),
            dma((5, share)),
        ]
    )
    return pl.pallas_call(
        functools.partial(steps_kernel, tiles, groups),
        in_specs=[smem] * (1 + len(scalars)) + [vmem, anywhere],
        out_specs=[vmem, vmem],
        out_shape=[
            pltpu.VMEM((local_dirs, bands, wide, high, deep), jnp.float32),
            jax.ShapeDtypeStruct((rows, deep), jnp.float32),
        ],
        scratch_shapes=scratch,
        compiler_params=pltpu.CompilerParams(
            collective_id=0, has_side_effects=True, vmem_limit_bytes=52 << 20
        ),
    )(position, *scalars, facets, home)


def beam_coeffs(abs_speed):
    return (
        1.0 - 1.5 * abs_speed + 0.5 * abs_speed * abs_speed,
        2.0 * abs_speed - abs_speed * abs_speed,
        0.5 * abs_speed * abs_speed - 0.5 * abs_speed,
    )


def on_device(
    phonon_heat_density,
    directions,
    quad_weight,
    mirror,
    band_courant,
    relax_rate,
    mode_heat_magnitude,
    mode_pulsation,
    wall_blocks,
    wall_count,
    wall_facet,
):
    local_dirs, bands, wide, high, deep = phonon_heat_density.shape
    tiles, groups = lax.axis_size("space"), lax.axis_size("dir")
    rows = wide * high
    share = -(-bands // groups)
    extra = share * groups - bands

    order, position = orbit_order(directions, mirror)
    own_facets = facet_grid(
        wall_blocks[0], wall_count[0], wall_facet[0], wide * high * deep // BLOCK
    ).astype(jnp.float32)
    home = phonon_heat_density
    if extra:
        home = jnp.pad(home, ((0, 0), (0, extra), (0, 0), (0, 0), (0, 0)))
    scalars = (
        order,
        directions,
        quad_weight,
        band_courant,
        relax_rate,
        mode_heat_magnitude,
        mode_pulsation,
    )
    out, kelvin = steps(
        tiles, groups, share, position, scalars, own_facets.reshape(rows, deep), home
    )
    return out, kelvin.reshape(wide, high, deep)


def solution(mesh):
    in_specs = (
        P("dir", None, "space", None, None),
        P(),
        P(),
        P(),
        P(),
        P(),
        P(),
        P(),
        P("space", None),
        P("space"),
        P("space", None, None),
    )
    out_specs = (P("dir", None, "space", None, None), P("space", None, None))
    return jax.shard_map(
        on_device, mesh=mesh, in_specs=in_specs, out_specs=out_specs, check_vma=False
    )
```

```python
import functools

import jax
import jax.numpy as jnp
from jax import lax
from jax.experimental import pallas as pl
from jax.experimental.pallas import tpu as pltpu
from jax.sharding import PartitionSpec as P

NEWTON = 4
BLOCK = 128
OCT = 8


def flat(values, axis):
    return jnp.sum(values, axis=axis, keepdims=True)


def orbit_order(directions, mirror):
    count = directions.shape[1]
    lane = lax.broadcasted_iota(jnp.int32, (count, count), 1).astype(jnp.float32)
    line = lax.broadcasted_iota(jnp.int32, (count, count), 0).astype(jnp.float32)
    same = lane == line
    positive = [jnp.where(directions[a : a + 1] > 0, 1.0, 0.0) for a in range(3)]
    code = positive[0] + 2.0 * positive[1] + 4.0 * positive[2]
    rep = flat(jnp.where(same, lane, 0.0), 1)
    for a in range(3):
        partner = mirror[a : a + 1].astype(jnp.float32)
        flipped = flat(jnp.where(rep == lane, partner, 0.0), 1)
        ahead = flat(jnp.where(same, positive[a], 0.0), 1)
        rep = jnp.where(ahead > 0.5, rep, flipped)
    rank = flat(jnp.where(lane < rep, jnp.where(code == OCT - 1, 1.0, 0.0), 0.0), 1)
    position = OCT * rank + flat(jnp.where(same, code, 0.0), 1)
    order = flat(jnp.where(position == lane, line, 0.0), 0)
    position = flat(jnp.where(same, position, 0.0), 0)
    return [jnp.clip(v.astype(jnp.int32), 0, count - 1) for v in (order, position)]


def facet_grid(blocks_ref, count_ref, wall_ref, rows, deep):
    cuts = deep // BLOCK
    row_id = lax.broadcasted_iota(jnp.int32, (rows, BLOCK), 0)
    grid = []
    for h in range(cuts):
        facets = jnp.zeros((rows, BLOCK), jnp.int32)
        for slot in range(wall_ref.shape[1]):
            block = jnp.where(slot < count_ref[0], blocks_ref[0, slot], -1)
            facets = jnp.where(
                row_id * cuts + h == block, wall_ref[0, slot : slot + 1, :], facets
            )
        grid.append(facets.astype(jnp.float32))
    return grid


def roll(u, by, axis):
    return pltpu.roll(u, by % u.shape[axis], axis)


def unit_coeffs(scalars, band, orbit):
    order_ref, directions_ref, weight_ref, courant_ref, rate_ref = scalars
    bands = courant_ref.shape[0]
    real = band < bands
    index = jnp.minimum(band, bands - 1)
    courant, rate = courant_ref[index], jnp.where(real, rate_ref[index], 0.0)
    rep = order_ref[0, orbit * OCT + OCT - 1]
    coef = []
    for axis_num in range(3):
        coef.extend(beam_coeffs(courant * jnp.abs(directions_ref[axis_num, rep])))
    coef.append(rate * weight_ref[rep])
    return coef, rate


def surplus_of(q):
    series = jnp.ones_like(q)
    for n in range(9, 1, -1):
        series = 1.0 + series * (q * (1.0 / n))
    return jnp.where(q < 0.5, q * series, jnp.exp(q) - 1.0)


def newton(rate_ref, magnitude_ref, pulsation_ref, source):
    kelvin = jnp.ones_like(source)
    for newton_turn in range(NEWTON):
        inverse = 1.0 / kelvin

        def one(b, carry):
            mismatch, gradient = carry
            factor = rate_ref[b] * magnitude_ref[b]
            q = pulsation_ref[b] * inverse
            surplus = surplus_of(q)
            ratio = 1.0 / surplus
            term = factor * ratio
            return mismatch + term, gradient + term * q * ((surplus + 1.0) * ratio)

        zero = jnp.zeros_like(source)
        mismatch, gradient = lax.fori_loop(0, rate_ref.shape[0], one, (zero, zero), unroll=8)
        mismatch, gradient = mismatch - source, gradient * inverse
        kelvin = jnp.clip(kelvin - mismatch / gradient, 0.5 * kelvin, 2.0 * kelvin)
    return kelvin


def sweep_unit(high, tiles, coef, facets_ref, load, store):
    _, rows, width = facets_ref.shape
    row_id = lax.broadcasted_iota(jnp.int32, (rows, width), 0)
    height = row_id % high
    total = [jnp.zeros((rows, width), jnp.float32) for _ in range(tiles)]
    for o in range(OCT):
        way = [1 if o >> a & 1 else -1 for a in range(3)]
        cells = []
        for t in range(tiles):
            facets = facets_ref[t]
            u = load(t, o)
            for a in range(3):
                facing = float(2 * a + 1 if way[a] > 0 else 2 * a + 2)
                u = jnp.where(facets == facing, load(t, o ^ (1 << a)), u)
            cells.append(u)
        turned = [roll(u, high * way[0], 0) for u in cells]
        for t in range(tiles):
            up = (t - way[0]) % tiles
            edge = row_id < high if way[0] > 0 else row_id >= rows - high
            near = jnp.where(edge, turned[up], turned[t])
            u = coef[0] * cells[t] + coef[1] * near + coef[2] * cells[up]
            u = coef[3] * u + coef[4] * roll(u, way[1], 1) + coef[5] * roll(u, 2 * way[1], 1)
            wrap1 = height < 1 if way[2] > 0 else height >= high - 1
            wrap2 = height < 2 if way[2] > 0 else height >= high - 2
            near = jnp.where(wrap1, roll(u, (1 - high) * way[2], 0), roll(u, way[2], 0))
            far = jnp.where(wrap2, roll(u, (2 - high) * way[2], 0), roll(u, 2 * way[2], 0))
            u = coef[6] * u + coef[7] * near + coef[8] * far
            store(t, o, u)
            total[t] = total[t] + u
    return [coef[9] * total[t] for t in range(tiles)]


MESH = pl.DeviceIdType.MESH


def greet(tile, tiles, group, groups):
    barrier = pltpu.get_barrier_semaphore()
    for u in range(1, tiles):
        pl.semaphore_signal(
            barrier, inc=1, device_id=(lax.rem(tile + u, tiles), group), device_id_type=MESH
        )
    for t in range(1, groups):
        pl.semaphore_signal(
            barrier, inc=1, device_id=(tile, lax.rem(group + t, groups)), device_id_type=MESH
        )
    pl.semaphore_wait(barrier, tiles + groups - 2)


def remote(src, dst, send, recv, device):
    return pltpu.make_async_remote_copy(
        src_ref=src, dst_ref=dst, send_sem=send, recv_sem=recv, device_id=device, device_id_type=MESH
    )


WAYS = (1, 2, -1, -2)
UNROLL = 8


def steps_kernel(
    tiles, groups, directions_ref, weight_ref, courant_ref, rate_ref, magnitude_ref, pulsation_ref,
    blocks_ref, count_ref, vectors_ref, mirror_ref, wall_ref, home_ref, out_ref, kelvin_ref, *scratch
):
    local_dirs, slots, wide, high, deep = home_ref.shape
    share, rows, bands = slots // groups, wide * high, courant_ref.shape[0]
    dirs = local_dirs * groups
    part = dirs // tiles
    orbits = part // OCT
    landed, sorted_refs, fields, swept, back, unsorted = (
        scratch[n * share : (n + 1) * share] for n in range(6)
    )
    (
        order_ref, position_ref, ids_ref, facet_ref, coef_ref, home_back, between, facets_ref, source_ref, near, summed, far, found, shared, kelvins,
        dir_send, dir_recv, tile_send, tile_recv, rev_send, rev_recv, ret_send, ret_recv,
        facet_send, facet_recv, near_send, near_recv, far_send, far_recv, last_send, last_recv, own_sem,
    ) = scratch[6 * share :]
    scalars = (order_ref, directions_ref, weight_ref, courant_ref, rate_ref)
    tile, group = lax.axis_index("space"), lax.axis_index("dir")

    def to_tiles(u):
        return (lax.rem(tile + u, tiles), group)

    def to_groups(t):
        return (tile, lax.rem(group + t, groups))

    own = [
        pltpu.make_async_copy(
            home_ref.at[:, group * share + k],
            landed[k].at[pl.ds(group * local_dirs, local_dirs)],
            own_sem.at[0, k],
        )
        for k in range(share)
    ]
    for copy in own:
        copy.start()
    greet(tile, tiles, group, groups)

    first = []
    for k in range(share):
        line = []
        for t in range(1, groups):
            peer = lax.rem(group + t, groups)
            copy = remote(
                home_ref.at[:, peer * share + k],
                landed[k].at[pl.ds(group * local_dirs, local_dirs)],
                dir_send.at[k, t],
                dir_recv.at[k, t],
                to_groups(t),
            )
            copy.start()
            line.append(copy)
        first.append(line)

    order, position = orbit_order(vectors_ref[...], mirror_ref[...])
    ids_ref[0] = order
    ids_ref[1] = position
    tables = [
        pltpu.make_async_copy(ids_ref.at[0], order_ref, own_sem.at[5, 0]),
        pltpu.make_async_copy(ids_ref.at[1], position_ref, own_sem.at[6, 0]),
    ]
    for copy in tables:
        copy.start()
    for h, facets in enumerate(facet_grid(blocks_ref, count_ref, wall_ref, rows, deep)):
        facet_ref[:, h * BLOCK : (h + 1) * BLOCK] = facets
    own_facets = pltpu.make_async_copy(facet_ref, facets_ref.at[tile], own_sem.at[4, 0])
    own_facets.start()
    third = []
    for u in range(1, tiles):
        copy = remote(
            facet_ref, facets_ref.at[tile], facet_send.at[u], facet_recv.at[u], to_tiles(u)
        )
        copy.start()
        third.append(copy)
    source_ref[...] = jnp.zeros_like(source_ref)

    second, fourth, fifth = [], [], []
    turns = sorted(set(n % high for n in WAYS) - {0})
    width = 12 + len(turns)

    def table(b, carry):
        def one(d, carry):
            index, base = group * local_dirs + d, (b * local_dirs + d) * width
            line = []
            for a in range(3):
                line.append(both_ways(courant_ref[b] * directions_ref[a, index]))
            cz = [line[2][0]] + [0.0] * len(turns)
            for n, c in zip(WAYS, line[2][1:]):
                at = turns.index(n % high) + 1 if n % high else 0
                cz[at] = cz[at] + c
            values = list(line[0]) + list(line[1]) + cz
            values.append(rate_ref[b] * rate_ref[b] * weight_ref[index])
            for n, value in enumerate(values):
                coef_ref[base + n] = value
            return carry

        return lax.fori_loop(0, local_dirs, one, carry)

    lax.fori_loop(0, bands, table, 0)
    for copy in tables:
        copy.wait()

    def gather(k):
        own[k].wait()
        for copy in first[k]:
            copy.wait_recv()

        def move(j, carry):
            d = order_ref[0, j]
            for x in range(wide):
                sorted_refs[k][j, x * high : (x + 1) * high, :] = landed[k][d, x]
            return carry

        lax.fori_loop(0, dirs, move, 0, unroll=4)
        line = [
            pltpu.make_async_copy(
                sorted_refs[k].at[pl.ds(tile * part, part)], fields[k].at[tile], own_sem.at[1, k]
            )
        ]
        for u in range(1, tiles):
            peer = lax.rem(tile + u, tiles)
            line.append(
                remote(
                    sorted_refs[k].at[pl.ds(peer * part, part)],
                    fields[k].at[tile],
                    tile_send.at[k, u],
                    tile_recv.at[k, u],
                    to_tiles(u),
                )
            )
        for copy in line:
            copy.start()
        second.append(line)

    def sweep(k):
        second[k][0].wait()
        for copy in second[k][1:]:
            copy.wait_recv()

        def one(orbit, carry):
            coef, rate = unit_coeffs(scalars, group * share + k, tile * orbits + orbit)

            def keep_between(t, o, u):
                between[t, o] = u

            sums = sweep_unit(
                high, tiles, coef, facets_ref, lambda t, o: fields[k][t, orbit * OCT + o], keep_between
            )
            for t in range(tiles):
                source_ref[0, t] = source_ref[0, t] + sums[t]
            left = 1.0 - rate
            coef = coef[:6] + [left * c for c in coef[6:9]] + coef[9:]

            def keep_swept(t, o, u):
                swept[k][t, orbit * OCT + o] = left * u

            sums = sweep_unit(
                high, tiles, coef, facets_ref, lambda t, o: between[t, o], keep_swept
            )
            for t in range(tiles):
                source_ref[1, t] = source_ref[1, t] + sums[t]
            return carry

        lax.fori_loop(0, orbits, one, 0)

    def turn(k):
        line = [
            pltpu.make_async_copy(
                swept[k].at[tile], back[k].at[pl.ds(tile * part, part)], own_sem.at[2, k]
            )
        ]
        for u in range(1, tiles):
            peer = lax.rem(tile + u, tiles)
            line.append(
                remote(
                    swept[k].at[peer],
                    back[k].at[pl.ds(tile * part, part)],
                    rev_send.at[k, u],
                    rev_recv.at[k, u],
                    to_tiles(u),
                )
            )
        for copy in line:
            copy.start()
        fourth.append(line)

    def scatter(k):
        fourth[k][0].wait()
        for copy in fourth[k][1:]:
            copy.wait_recv()

        def move(d, carry):
            j = position_ref[0, d]
            for x in range(wide):
                unsorted[k][d, x] = back[k][j, x * high : (x + 1) * high, :]
            return carry

        lax.fori_loop(0, dirs, move, 0, unroll=4)

    def send_home(k):
        line = [
            pltpu.make_async_copy(
                unsorted[k].at[pl.ds(group * local_dirs, local_dirs)],
                home_back.at[:, group * share + k],
                own_sem.at[3, k],
            )
        ]
        for t in range(1, groups):
            peer = lax.rem(group + t, groups)
            line.append(
                remote(
                    unsorted[k].at[pl.ds(peer * local_dirs, local_dirs)],
                    home_back.at[:, group * share + k],
                    ret_send.at[k, t],
                    ret_recv.at[k, t],
                    to_groups(t),
                )
            )
        for copy in line:
            copy.start()
        fifth.append(line)

    def sum_groups(n):
        copies = []
        for t in range(1, groups):
            copy = remote(
                summed.at[n], far.at[n, group], far_send.at[n, t], far_recv.at[n, t], to_groups(t)
            )
            copy.start()
            copies.append(copy)
        far[n, group] = summed[n]
        return copies

    def total_of(n, copies):
        for copy in copies:
            copy.wait_recv()
        value = far[n, 0]
        for g in range(1, groups):
            value = value + far[n, g]
        return newton(rate_ref, magnitude_ref, pulsation_ref, value)

    last, early = share - 1, max(share - 3, 0)
    for k in range(share):
        gather(k)
        if k == 0:
            own_facets.wait()
            for copy in third:
                copy.wait_recv()
        else:
            sweep(k - 1)
            if k - 1 < early:
                turn(k - 1)
        if 2 <= k < early + 2:
            scatter(k - 2)
            send_home(k - 2)
    sweep(last)

    nears = []
    for u in range(1, tiles):
        peer = lax.rem(tile + u, tiles)
        copy = remote(
            source_ref.at[:, peer], near.at[u], near_send.at[u], near_recv.at[u], to_tiles(u)
        )
        copy.start()
        nears.append(copy)
    for k in range(early, last):
        turn(k)
    value = source_ref[:, tile]
    for u in range(1, tiles):
        nears[u - 1].wait_recv()
        value = value + near[u]
    summed[...] = value
    fars = sum_groups(0)
    while len(fifth) < share - 1:
        scatter(len(fifth))
        send_home(len(fifth))
    value = total_of(0, fars)
    shared[...] = value
    lasts = []
    for u in range(1, tiles):
        copy = remote(
            shared, kelvins.at[tile], last_send.at[u], last_recv.at[u], to_tiles(u)
        )
        copy.start()
        lasts.append(copy)
    kelvins[tile] = value
    turn(last)
    for copy in lasts:
        copy.wait_recv()

    below, above = lax.rem(tile + tiles - 1, tiles), lax.rem(tile + 1, tiles)
    row_id = lax.broadcasted_iota(jnp.int32, (rows, deep), 0)
    height = row_id % high

    def spin(u, n):
        return jnp.where(height < n, roll(u, n - high, 0), roll(u, n, 0))

    def drift_coeffs(d, b):
        base = (b * local_dirs + d) * width
        values = [coef_ref[base + n] for n in range(width)]
        return values[:5], values[5:10], values[10:-1], values[-1]

    def drift(b, acc):
        left = (1.0 - rate_ref[b]) * rate_ref[b]

        def bose(t):
            return magnitude_ref[b] / surplus_of(pulsation_ref[b] / kelvins[t])

        mine, low, up = bose(tile), bose(below), bose(above)
        shifted = [
            mine,
            jnp.where(row_id < high, roll(low, high, 0), roll(mine, high, 0)),
            low,
            jnp.where(row_id >= rows - high, roll(up, -high, 0), roll(mine, -high, 0)),
            up,
        ]

        def one(d, acc):
            cx, cy, cz, weight = drift_coeffs(d, b)
            u = combine(cx, shifted)
            u = combine(cy, [u] + [roll(u, n, 1) for n in WAYS])
            u = combine(cz, [u] + [spin(u, n) for n in turns])
            kept = left * u
            for x in range(wide):
                out_ref[d, b, x] = kept[x * high : (x + 1) * high]
            return acc + weight * u

        return lax.fori_loop(0, local_dirs, one, acc, unroll=UNROLL)

    acc = lax.fori_loop(0, bands, drift, jnp.zeros((rows, deep), jnp.float32))
    summed[1] = summed[1] + acc
    fars = fars + sum_groups(1)
    scatter(last)
    send_home(last)
    value = total_of(1, fars[groups - 1 :])
    found[...] = value
    for x in range(wide):
        kelvin_ref[x] = value[x * high : (x + 1) * high]

    def settle(b, carry):
        heat = rate_ref[b] * (magnitude_ref[b] / surplus_of(pulsation_ref[b] / found[...]))

        def one(d, carry):
            for x in range(wide):
                out_ref[d, b, x] = out_ref[d, b, x] + heat[x * high : (x + 1) * high]
            return carry

        return lax.fori_loop(0, local_dirs, one, carry, unroll=4)

    lax.fori_loop(0, bands, settle, 0)
    for k in range(share):
        fifth[k][0].wait()
        for copy in fifth[k][1:]:
            copy.wait_recv()

        def one(d, carry):
            for g in range(groups):
                b = g * share + k
                if b < bands:
                    for x in range(wide):
                        out_ref[d, b, x] = out_ref[d, b, x] + home_back[d, b, x]
            return carry

        lax.fori_loop(0, local_dirs, one, 0, unroll=2)
    for copy in third + nears + fars + lasts:
        copy.wait_send()
    for line in first:
        for copy in line:
            copy.wait_send()
    for line in second + fourth + fifth:
        for copy in line[1:]:
            copy.wait_send()


def both_ways(speed):
    centre, near, far = beam_coeffs(jnp.abs(speed))
    forward = speed > 0
    return (
        centre,
        jnp.where(forward, near, 0.0),
        jnp.where(forward, far, 0.0),
        jnp.where(forward, 0.0, near),
        jnp.where(forward, 0.0, far),
    )


def combine(coef, moves):
    total = coef[0] * moves[0]
    for c, move in zip(coef[1:], moves[1:]):
        total = total + c * move
    return total


def steps(tiles, groups, share, scalars, walls, vectors, home):
    local_dirs, _, wide, high, deep = home.shape
    dirs, rows = local_dirs * groups, wide * high
    part = dirs // tiles
    bands = scalars[2].shape[0]
    vmem = pl.BlockSpec(memory_space=pltpu.VMEM)
    smem = pl.BlockSpec(memory_space=pltpu.SMEM)
    anywhere = pl.BlockSpec(memory_space=pl.ANY)
    dma = pltpu.SemaphoreType.DMA
    scratch = (
        [pltpu.VMEM((dirs, wide, high, deep), jnp.float32)] * share
        + [pltpu.VMEM((dirs, rows, deep), jnp.float32)] * share
        + [pltpu.VMEM((tiles, part, rows, deep), jnp.float32)] * (2 * share)
        + [pltpu.VMEM((dirs, rows, deep), jnp.float32)] * share
        + [pltpu.VMEM((dirs, wide, high, deep), jnp.float32)] * share
        + [
            pltpu.SMEM((1, dirs), jnp.int32),
            pltpu.SMEM((1, dirs), jnp.int32),
            pltpu.VMEM((2, 1, dirs), jnp.int32),
            pltpu.VMEM((rows, deep), jnp.float32),
            pltpu.SMEM((bands * local_dirs * (12 + len(set(n % high for n in WAYS) - {0})),), jnp.float32),
            pltpu.VMEM((local_dirs, share * groups, wide, high, deep), jnp.float32),
            pltpu.VMEM((tiles, OCT, rows, deep), jnp.float32),
            pltpu.VMEM((tiles, rows, deep), jnp.float32),
            pltpu.VMEM((2, tiles, rows, deep), jnp.float32),
            pltpu.VMEM((tiles, 2, rows, deep), jnp.float32),
            pltpu.VMEM((2, rows, deep), jnp.float32),
            pltpu.VMEM((2, groups, rows, deep), jnp.float32),
            pltpu.VMEM((rows, deep), jnp.float32),
            pltpu.VMEM((rows, deep), jnp.float32),
            pltpu.VMEM((tiles, rows, deep), jnp.float32),
            dma((share, groups)),
            dma((share, groups)),
            dma((share, tiles)),
            dma((share, tiles)),
            dma((share, tiles)),
            dma((share, tiles)),
            dma((share, groups)),
            dma((share, groups)),
            dma((tiles,)),
            dma((tiles,)),
            dma((tiles,)),
            dma((tiles,)),
            dma((2, groups)),
            dma((2, groups)),
            dma((tiles,)),
            dma((tiles,)),
            dma((7, share)),
        ]
    )
    return pl.pallas_call(
        functools.partial(steps_kernel, tiles, groups),
        in_specs=[smem] * (len(scalars) + 2) + [vmem] * 3 + [anywhere],
        out_specs=[vmem, vmem],
        out_shape=[
            pltpu.VMEM((local_dirs, bands, wide, high, deep), jnp.float32),
            jax.ShapeDtypeStruct((wide, high, deep), jnp.float32),
        ],
        scratch_shapes=scratch,
        compiler_params=pltpu.CompilerParams(
            collective_id=0, has_side_effects=True, vmem_limit_bytes=52 << 20
        ),
    )(*scalars, *walls[:2], *vectors, walls[2], home)


def beam_coeffs(abs_speed):
    return (
        1.0 - 1.5 * abs_speed + 0.5 * abs_speed * abs_speed,
        2.0 * abs_speed - abs_speed * abs_speed,
        0.5 * abs_speed * abs_speed - 0.5 * abs_speed,
    )


def on_device(
    phonon_heat_density,
    directions,
    quad_weight,
    mirror,
    band_courant,
    relax_rate,
    mode_heat_magnitude,
    mode_pulsation,
    wall_blocks,
    wall_count,
    wall_facet,
):
    local_dirs, bands, wide, high, deep = phonon_heat_density.shape
    tiles, groups = lax.axis_size("space"), lax.axis_size("dir")
    share = -(-bands // groups)
    extra = share * groups - bands
    home = phonon_heat_density
    if extra:
        home = jnp.pad(home, ((0, 0), (0, extra), (0, 0), (0, 0), (0, 0)))
    scalars = (
        directions,
        quad_weight,
        band_courant,
        relax_rate,
        mode_heat_magnitude,
        mode_pulsation,
    )
    walls = (wall_blocks, wall_count, wall_facet)
    return steps(tiles, groups, share, scalars, walls, (directions, mirror), home)


def solution(mesh):
    in_specs = (
        P("dir", None, "space", None, None),
        P(),
        P(),
        P(),
        P(),
        P(),
        P(),
        P(),
        P("space", None),
        P("space"),
        P("space", None, None),
    )
    out_specs = (P("dir", None, "space", None, None), P("space", None, None))
    return jax.shard_map(
        on_device, mesh=mesh, in_specs=in_specs, out_specs=out_specs, check_vma=False
    )
```

```python
import functools

import jax
import jax.numpy as jnp
from jax import lax
from jax.experimental import pallas as pl
from jax.experimental.pallas import tpu as pltpu
from jax.sharding import PartitionSpec as P

NEWTON = 4
BLOCK = 128
OCT = 8


def flat(values, axis):
    return jnp.sum(values, axis=axis, keepdims=True)


def orbit_order(directions, mirror):
    count = directions.shape[1]
    lane = lax.broadcasted_iota(jnp.int32, (count, count), 1).astype(jnp.float32)
    line = lax.broadcasted_iota(jnp.int32, (count, count), 0).astype(jnp.float32)
    same = lane == line
    positive = [jnp.where(directions[a : a + 1] > 0, 1.0, 0.0) for a in range(3)]
    code = positive[0] + 2.0 * positive[1] + 4.0 * positive[2]
    rep = flat(jnp.where(same, lane, 0.0), 1)
    for a in range(3):
        partner = mirror[a : a + 1].astype(jnp.float32)
        flipped = flat(jnp.where(rep == lane, partner, 0.0), 1)
        ahead = flat(jnp.where(same, positive[a], 0.0), 1)
        rep = jnp.where(ahead > 0.5, rep, flipped)
    rank = flat(jnp.where(lane < rep, jnp.where(code == OCT - 1, 1.0, 0.0), 0.0), 1)
    position = OCT * rank + flat(jnp.where(same, code, 0.0), 1)
    order = flat(jnp.where(position == lane, line, 0.0), 0)
    position = flat(jnp.where(same, position, 0.0), 0)
    return [jnp.clip(v.astype(jnp.int32), 0, count - 1) for v in (order, position)]


def facet_grid(blocks_ref, count_ref, wall_ref, rows, deep):
    cuts = deep // BLOCK
    row_id = lax.broadcasted_iota(jnp.int32, (rows, BLOCK), 0)
    grid = []
    for h in range(cuts):
        facets = jnp.zeros((rows, BLOCK), jnp.int32)
        for slot in range(wall_ref.shape[1]):
            block = jnp.where(slot < count_ref[0], blocks_ref[0, slot], -1)
            facets = jnp.where(
                row_id * cuts + h == block, wall_ref[0, slot : slot + 1, :], facets
            )
        grid.append(facets.astype(jnp.float32))
    return grid


def roll(u, by, axis):
    return pltpu.roll(u, by % u.shape[axis], axis)


def unit_coeffs(scalars, band, orbit):
    order_ref, directions_ref, weight_ref, courant_ref, rate_ref = scalars
    bands = courant_ref.shape[0]
    real = band < bands
    index = jnp.minimum(band, bands - 1)
    courant, rate = courant_ref[index], jnp.where(real, rate_ref[index], 0.0)
    rep = order_ref[0, orbit * OCT + OCT - 1]
    coef = []
    for axis_num in range(3):
        coef.extend(beam_coeffs(courant * jnp.abs(directions_ref[axis_num, rep])))
    coef.append(rate * weight_ref[rep])
    return coef, rate


def surplus_of(q):
    series = jnp.ones_like(q)
    for n in range(9, 1, -1):
        series = 1.0 + series * (q * (1.0 / n))
    return jnp.where(q < 0.5, q * series, jnp.exp(q) - 1.0)


def newton(rate_ref, magnitude_ref, pulsation_ref, source):
    kelvin = jnp.ones_like(source)
    for newton_turn in range(NEWTON):
        inverse = 1.0 / kelvin

        def one(b, carry):
            mismatch, gradient = carry
            factor = rate_ref[b] * magnitude_ref[b]
            q = pulsation_ref[b] * inverse
            surplus = surplus_of(q)
            ratio = 1.0 / surplus
            term = factor * ratio
            return mismatch + term, gradient + term * q * ((surplus + 1.0) * ratio)

        zero = jnp.zeros_like(source)
        mismatch, gradient = lax.fori_loop(0, rate_ref.shape[0], one, (zero, zero), unroll=8)
        mismatch, gradient = mismatch - source, gradient * inverse
        kelvin = jnp.clip(kelvin - mismatch / gradient, 0.5 * kelvin, 2.0 * kelvin)
    return kelvin


def sweep_unit(high, tiles, coef, facets_ref, load, store):
    _, rows, width = facets_ref.shape
    row_id = lax.broadcasted_iota(jnp.int32, (rows, width), 0)
    height = row_id % high
    total = [jnp.zeros((rows, width), jnp.float32) for _ in range(tiles)]
    for o in range(OCT):
        way = [1 if o >> a & 1 else -1 for a in range(3)]
        cells = []
        for t in range(tiles):
            facets = facets_ref[t]
            u = load(t, o)
            for a in range(3):
                facing = float(2 * a + 1 if way[a] > 0 else 2 * a + 2)
                u = jnp.where(facets == facing, load(t, o ^ (1 << a)), u)
            cells.append(u)
        turned = [roll(u, high * way[0], 0) for u in cells]
        for t in range(tiles):
            up = (t - way[0]) % tiles
            edge = row_id < high if way[0] > 0 else row_id >= rows - high
            near = jnp.where(edge, turned[up], turned[t])
            u = coef[0] * cells[t] + coef[1] * near + coef[2] * cells[up]
            u = coef[3] * u + coef[4] * roll(u, way[1], 1) + coef[5] * roll(u, 2 * way[1], 1)
            wrap1 = height < 1 if way[2] > 0 else height >= high - 1
            wrap2 = height < 2 if way[2] > 0 else height >= high - 2
            near = jnp.where(wrap1, roll(u, (1 - high) * way[2], 0), roll(u, way[2], 0))
            far = jnp.where(wrap2, roll(u, (2 - high) * way[2], 0), roll(u, 2 * way[2], 0))
            u = coef[6] * u + coef[7] * near + coef[8] * far
            store(t, o, u)
            total[t] = total[t] + u
    return [coef[9] * total[t] for t in range(tiles)]


MESH = pl.DeviceIdType.MESH


def greet(tile, tiles, group, groups):
    barrier = pltpu.get_barrier_semaphore()
    for u in range(1, tiles):
        pl.semaphore_signal(
            barrier, inc=1, device_id=(lax.rem(tile + u, tiles), group), device_id_type=MESH
        )
    for t in range(1, groups):
        pl.semaphore_signal(
            barrier, inc=1, device_id=(tile, lax.rem(group + t, groups)), device_id_type=MESH
        )
    pl.semaphore_wait(barrier, tiles + groups - 2)


def remote(src, dst, send, recv, device):
    return pltpu.make_async_remote_copy(
        src_ref=src, dst_ref=dst, send_sem=send, recv_sem=recv, device_id=device, device_id_type=MESH
    )


WAYS = (1, 2, -1, -2)
UNROLL = 8


def steps_kernel(
    tiles, groups, small, *refs
):
    given, (home_ref, out_ref, home_back, kelvin_ref) = refs[:small], refs[small : small + 4]
    held, scratch = refs[small + 4 : 2 * small + 4], refs[2 * small + 4 : -1]
    (
        directions_ref, weight_ref, courant_ref, rate_ref, magnitude_ref, pulsation_ref, blocks_ref,
        count_ref, vectors_ref, mirror_ref, wall_ref,
    ) = held
    inputs = [
        pltpu.make_async_copy(src, dst, refs[-1].at[n])
        for n, (src, dst) in enumerate(zip(given, held))
    ]
    local_dirs, slots, wide, high, deep = home_ref.shape
    share, rows, bands = slots // groups, wide * high, courant_ref.shape[0]
    dirs = local_dirs * groups
    part = dirs // tiles
    orbits = part // OCT
    landed, sorted_refs, fields, swept, back, unsorted = (
        scratch[n * share : (n + 1) * share] for n in range(6)
    )
    (
        order_ref, position_ref, ids_ref, facet_ref, coef_ref, between, facets_ref, source_ref, near, summed, far, found, shared, kelvins,
        dir_send, dir_recv, tile_send, tile_recv, rev_send, rev_recv, ret_send, ret_recv,
        facet_send, facet_recv, near_send, near_recv, far_send, far_recv, last_send, last_recv, own_sem,
    ) = scratch[6 * share :]
    scalars = (order_ref, directions_ref, weight_ref, courant_ref, rate_ref)
    tile, group = lax.axis_index("space"), lax.axis_index("dir")

    def to_tiles(u):
        return (lax.rem(tile + u, tiles), group)

    def other(t):
        if groups & (groups - 1):
            return lax.rem(group + t, groups)
        return lax.bitwise_xor(group, t)

    def sender(t):
        if groups & (groups - 1):
            return lax.rem(group + groups - t, groups)
        return lax.bitwise_xor(group, t)

    def to_groups(t):
        return (tile, other(t))

    own = [
        pltpu.make_async_copy(
            home_ref.at[:, group * share + k],
            landed[k].at[pl.ds(group * local_dirs, local_dirs)],
            own_sem.at[0, k],
        )
        for k in range(share)
    ]
    for copy in own + inputs:
        copy.start()
    greet(tile, tiles, group, groups)

    first = []
    for k in range(share):
        line = []
        for t in range(1, groups):
            peer = other(t)
            copy = remote(
                home_ref.at[:, peer * share + k],
                landed[k].at[pl.ds(group * local_dirs, local_dirs)],
                dir_send.at[k, t],
                dir_recv.at[k, t],
                to_groups(t),
            )
            copy.start()
            line.append(copy)
        first.append(line)

    for copy in inputs:
        copy.wait()
    order, position = orbit_order(vectors_ref[...], mirror_ref[...])
    ids_ref[0] = order
    ids_ref[1] = position
    tables = [
        pltpu.make_async_copy(ids_ref.at[0], order_ref, own_sem.at[5, 0]),
        pltpu.make_async_copy(ids_ref.at[1], position_ref, own_sem.at[6, 0]),
    ]
    for copy in tables:
        copy.start()
    for h, facets in enumerate(facet_grid(blocks_ref, count_ref, wall_ref, rows, deep)):
        facet_ref[:, h * BLOCK : (h + 1) * BLOCK] = facets
    own_facets = pltpu.make_async_copy(facet_ref, facets_ref.at[tile], own_sem.at[4, 0])
    own_facets.start()
    third = []
    for u in range(1, tiles):
        copy = remote(
            facet_ref, facets_ref.at[tile], facet_send.at[u], facet_recv.at[u], to_tiles(u)
        )
        copy.start()
        third.append(copy)
    source_ref[...] = jnp.zeros_like(source_ref)

    second, fourth, fifth = [], [], []
    turns = sorted(set(n % high for n in WAYS) - {0})
    width = 12 + len(turns)

    def table(b, carry):
        def one(d, carry):
            index, base = group * local_dirs + d, (b * local_dirs + d) * width
            line = []
            for a in range(3):
                line.append(both_ways(courant_ref[b] * directions_ref[a, index]))
            cz = [line[2][0]] + [0.0] * len(turns)
            for n, c in zip(WAYS, line[2][1:]):
                at = turns.index(n % high) + 1 if n % high else 0
                cz[at] = cz[at] + c
            values = list(line[0]) + list(line[1]) + cz
            values.append(rate_ref[b] * rate_ref[b] * weight_ref[index])
            for n, value in enumerate(values):
                coef_ref[base + n] = value
            return carry

        return lax.fori_loop(0, local_dirs, one, carry)

    lax.fori_loop(0, bands, table, 0)
    for copy in tables:
        copy.wait()

    def gather(k):
        own[k].wait()
        for copy in first[k]:
            copy.wait_recv()

        def move(j, carry):
            d = order_ref[0, j]
            for x in range(wide):
                sorted_refs[k][j, x * high : (x + 1) * high, :] = landed[k][d, x]
            return carry

        lax.fori_loop(0, dirs, move, 0, unroll=4)
        line = [
            pltpu.make_async_copy(
                sorted_refs[k].at[pl.ds(tile * part, part)], fields[k].at[tile], own_sem.at[1, k]
            )
        ]
        for u in range(1, tiles):
            peer = lax.rem(tile + u, tiles)
            line.append(
                remote(
                    sorted_refs[k].at[pl.ds(peer * part, part)],
                    fields[k].at[tile],
                    tile_send.at[k, u],
                    tile_recv.at[k, u],
                    to_tiles(u),
                )
            )
        for copy in line:
            copy.start()
        second.append(line)

    def sweep(k):
        second[k][0].wait()
        for copy in second[k][1:]:
            copy.wait_recv()

        def one(orbit, carry):
            coef, rate = unit_coeffs(scalars, group * share + k, tile * orbits + orbit)

            def keep_between(t, o, u):
                between[t, o] = u

            sums = sweep_unit(
                high, tiles, coef, facets_ref, lambda t, o: fields[k][t, orbit * OCT + o], keep_between
            )
            for t in range(tiles):
                source_ref[0, t] = source_ref[0, t] + sums[t]
            left = 1.0 - rate
            coef = coef[:6] + [left * c for c in coef[6:9]] + coef[9:]

            def keep_swept(t, o, u):
                swept[k][t, orbit * OCT + o] = left * u

            sums = sweep_unit(
                high, tiles, coef, facets_ref, lambda t, o: between[t, o], keep_swept
            )
            for t in range(tiles):
                source_ref[1, t] = source_ref[1, t] + sums[t]
            return carry

        lax.fori_loop(0, orbits, one, 0)

    def turn(k):
        line = [
            pltpu.make_async_copy(
                swept[k].at[tile], back[k].at[pl.ds(tile * part, part)], own_sem.at[2, k]
            )
        ]
        for u in range(1, tiles):
            peer = lax.rem(tile + u, tiles)
            line.append(
                remote(
                    swept[k].at[peer],
                    back[k].at[pl.ds(tile * part, part)],
                    rev_send.at[k, u],
                    rev_recv.at[k, u],
                    to_tiles(u),
                )
            )
        for copy in line:
            copy.start()
        fourth.append(line)

    def scatter(k):
        fourth[k][0].wait()
        for copy in fourth[k][1:]:
            copy.wait_recv()

        def move(d, carry):
            j = position_ref[0, d]
            for x in range(wide):
                unsorted[k][d, x] = back[k][j, x * high : (x + 1) * high, :]
            return carry

        lax.fori_loop(0, dirs, move, 0, unroll=4)

    def send_home(k):
        line = [
            pltpu.make_async_copy(
                unsorted[k].at[pl.ds(group * local_dirs, local_dirs)],
                home_back.at[:, group * share + k],
                own_sem.at[3, k],
            )
        ]
        for t in range(1, groups):
            peer = other(t)
            line.append(
                remote(
                    unsorted[k].at[pl.ds(peer * local_dirs, local_dirs)],
                    home_back.at[:, group * share + k],
                    ret_send.at[k, t],
                    ret_recv.at[k, t],
                    to_groups(t),
                )
            )
        for copy in line:
            copy.start()
        fifth.append(line)

    def sum_groups(n):
        copies = []
        for t in range(1, groups):
            copy = remote(
                summed.at[n], far.at[n, group], far_send.at[n, t], far_recv.at[n, t], to_groups(t)
            )
            copy.start()
            copies.append(copy)
        far[n, group] = summed[n]
        return copies

    def total_of(n, copies):
        for copy in copies:
            copy.wait_recv()
        value = far[n, 0]
        for g in range(1, groups):
            value = value + far[n, g]
        return newton(rate_ref, magnitude_ref, pulsation_ref, value)

    last, early = share - 1, max(share - 3, 0)
    for k in range(share):
        gather(k)
        if k == 0:
            own_facets.wait()
            for copy in third:
                copy.wait_recv()
        else:
            sweep(k - 1)
            if k - 1 < early:
                turn(k - 1)
        if 2 <= k < early + 2:
            scatter(k - 2)
            send_home(k - 2)
    sweep(last)

    nears = []
    for u in range(1, tiles):
        peer = lax.rem(tile + u, tiles)
        copy = remote(
            source_ref.at[:, peer], near.at[u], near_send.at[u], near_recv.at[u], to_tiles(u)
        )
        copy.start()
        nears.append(copy)
    for k in range(early, last):
        turn(k)
    value = source_ref[:, tile]
    for u in range(1, tiles):
        nears[u - 1].wait_recv()
        value = value + near[u]
    summed[...] = value
    fars = sum_groups(0)
    while len(fifth) < share - 1:
        scatter(len(fifth))
        send_home(len(fifth))
    value = total_of(0, fars)
    shared[...] = value
    lasts = []
    for u in range(1, tiles):
        copy = remote(
            shared, kelvins.at[tile], last_send.at[u], last_recv.at[u], to_tiles(u)
        )
        copy.start()
        lasts.append(copy)
    kelvins[tile] = value
    turn(last)
    for copy in lasts:
        copy.wait_recv()

    below, above = lax.rem(tile + tiles - 1, tiles), lax.rem(tile + 1, tiles)
    row_id = lax.broadcasted_iota(jnp.int32, (rows, deep), 0)
    height = row_id % high

    def spin(u, n):
        return jnp.where(height < n, roll(u, n - high, 0), roll(u, n, 0))

    def drift_coeffs(d, b):
        base = (b * local_dirs + d) * width
        values = [coef_ref[base + n] for n in range(width)]
        return values[:5], values[5:10], values[10:-1], values[-1]

    def drift(b, acc):
        left = (1.0 - rate_ref[b]) * rate_ref[b]

        def bose(t):
            return magnitude_ref[b] / surplus_of(pulsation_ref[b] / kelvins[t])

        mine, low, up = bose(tile), bose(below), bose(above)
        shifted = [
            mine,
            jnp.where(row_id < high, roll(low, high, 0), roll(mine, high, 0)),
            low,
            jnp.where(row_id >= rows - high, roll(up, -high, 0), roll(mine, -high, 0)),
            up,
        ]

        def one(d, acc):
            cx, cy, cz, weight = drift_coeffs(d, b)
            u = combine(cx, shifted)
            u = combine(cy, [u] + [roll(u, n, 1) for n in WAYS])
            u = combine(cz, [u] + [spin(u, n) for n in turns])
            kept = left * u
            for x in range(wide):
                out_ref[d, b, x] = kept[x * high : (x + 1) * high]
            return acc + weight * u

        return lax.fori_loop(0, local_dirs, one, acc, unroll=UNROLL)

    acc = lax.fori_loop(0, bands, drift, jnp.zeros((rows, deep), jnp.float32))
    summed[1] = summed[1] + acc
    fars = fars + sum_groups(1)
    scatter(last)
    send_home(last)
    value = total_of(1, fars[groups - 1 :])
    found[...] = value
    for x in range(wide):
        kelvin_ref[x] = value[x * high : (x + 1) * high]

    def settle(b, carry):
        heat = rate_ref[b] * (magnitude_ref[b] / surplus_of(pulsation_ref[b] / found[...]))

        def one(d, carry):
            for x in range(wide):
                out_ref[d, b, x] = out_ref[d, b, x] + heat[x * high : (x + 1) * high]
            return carry

        return lax.fori_loop(0, local_dirs, one, carry, unroll=4)

    lax.fori_loop(0, bands, settle, 0)
    for k in range(share):
        for t in range(groups):
            if t:
                fifth[k][t].wait_recv()
            else:
                fifth[k][0].wait()
            if k == last:
                continue
            b = sender(t) * share + k

            def one(d, carry):
                for x in range(wide):
                    out_ref[d, b, x] = out_ref[d, b, x] + home_back[d, b, x]
                return carry

            if share * groups == bands:
                lax.fori_loop(0, local_dirs, one, 0, unroll=8)
            else:
                lax.fori_loop(0, jnp.where(b < bands, local_dirs, 0), one, 0)
    for copy in third + nears + fars + lasts:
        copy.wait_send()
    for line in first:
        for copy in line:
            copy.wait_send()
    for line in second + fourth + fifth:
        for copy in line[1:]:
            copy.wait_send()


def settle_kernel(groups, sum_ref, home_back, kelvin_ref, out_ref, kelvin_out, last_ref, sems):
    local_dirs, bands, wide = sum_ref.shape[:3]
    share = home_back.shape[1] // groups
    copies = [pltpu.make_async_copy(kelvin_ref, kelvin_out, sems.at[2 * groups])]
    for g in range(groups):
        count = min(bands - g * share, share - 1)
        if count > 0:
            part = pl.ds(g * share, count)
            copies.append(
                pltpu.make_async_copy(sum_ref.at[:, part], out_ref.at[:, part], sems.at[g])
            )
    for copy in copies:
        copy.start()
    for g in range(groups):
        b = (g + 1) * share - 1
        if b < bands:

            def one(d, carry):
                for x in range(wide):
                    last_ref[g, d, x] = sum_ref[d, b, x] + home_back[d, b, x]
                return carry

            lax.fori_loop(0, local_dirs, one, 0, unroll=8)
            copy = pltpu.make_async_copy(last_ref.at[g], out_ref.at[:, b], sems.at[groups + g])
            copy.start()
            copies.append(copy)
    for copy in copies:
        copy.wait()


def both_ways(speed):
    centre, near, far = beam_coeffs(jnp.abs(speed))
    forward = speed > 0
    return (
        centre,
        jnp.where(forward, near, 0.0),
        jnp.where(forward, far, 0.0),
        jnp.where(forward, 0.0, near),
        jnp.where(forward, 0.0, far),
    )


def combine(coef, moves):
    total = coef[0] * moves[0]
    for c, move in zip(coef[1:], moves[1:]):
        total = total + c * move
    return total


def steps(tiles, groups, share, scalars, walls, vectors, home):
    local_dirs, _, wide, high, deep = home.shape
    dirs, rows = local_dirs * groups, wide * high
    part = dirs // tiles
    bands = scalars[2].shape[0]
    vmem = pl.BlockSpec(memory_space=pltpu.VMEM)
    anywhere = pl.BlockSpec(memory_space=pl.ANY)
    dma = pltpu.SemaphoreType.DMA
    scratch = (
        [pltpu.VMEM((dirs, wide, high, deep), jnp.float32)] * share
        + [pltpu.VMEM((dirs, rows, deep), jnp.float32)] * share
        + [pltpu.VMEM((tiles, part, rows, deep), jnp.float32)] * (2 * share)
        + [pltpu.VMEM((dirs, rows, deep), jnp.float32)] * share
        + [pltpu.VMEM((dirs, wide, high, deep), jnp.float32)] * share
        + [
            pltpu.SMEM((1, dirs), jnp.int32),
            pltpu.SMEM((1, dirs), jnp.int32),
            pltpu.VMEM((2, 1, dirs), jnp.int32),
            pltpu.VMEM((rows, deep), jnp.float32),
            pltpu.SMEM((bands * local_dirs * (12 + len(set(n % high for n in WAYS) - {0})),), jnp.float32),
            pltpu.VMEM((tiles, OCT, rows, deep), jnp.float32),
            pltpu.VMEM((tiles, rows, deep), jnp.float32),
            pltpu.VMEM((2, tiles, rows, deep), jnp.float32),
            pltpu.VMEM((tiles, 2, rows, deep), jnp.float32),
            pltpu.VMEM((2, rows, deep), jnp.float32),
            pltpu.VMEM((2, groups, rows, deep), jnp.float32),
            pltpu.VMEM((rows, deep), jnp.float32),
            pltpu.VMEM((rows, deep), jnp.float32),
            pltpu.VMEM((tiles, rows, deep), jnp.float32),
            dma((share, groups)),
            dma((share, groups)),
            dma((share, tiles)),
            dma((share, tiles)),
            dma((share, tiles)),
            dma((share, tiles)),
            dma((share, groups)),
            dma((share, groups)),
            dma((tiles,)),
            dma((tiles,)),
            dma((tiles,)),
            dma((tiles,)),
            dma((2, groups)),
            dma((2, groups)),
            dma((tiles,)),
            dma((tiles,)),
            dma((7, share)),
        ]
    )
    held = [pltpu.SMEM(v.shape, v.dtype) for v in (*scalars, *walls[:2])]
    held += [pltpu.VMEM(v.shape, v.dtype) for v in (*vectors, walls[2])]
    parts = pl.pallas_call(
        functools.partial(steps_kernel, tiles, groups, len(held)),
        in_specs=[anywhere] * (len(held) + 1),
        out_specs=[vmem] * 3,
        out_shape=[
            pltpu.VMEM((local_dirs, bands, wide, high, deep), jnp.float32),
            pltpu.VMEM((local_dirs, share * groups, wide, high, deep), jnp.float32),
            pltpu.VMEM((wide, high, deep), jnp.float32),
        ],
        scratch_shapes=held + scratch + [dma((len(held),))],
        compiler_params=pltpu.CompilerParams(
            collective_id=0, has_side_effects=True, vmem_limit_bytes=46 << 20
        ),
    )(*scalars, *walls[:2], *vectors, walls[2], home)
    return pl.pallas_call(
        functools.partial(settle_kernel, groups),
        in_specs=[vmem] * 3,
        out_specs=[anywhere] * 2,
        out_shape=[
            jax.ShapeDtypeStruct((local_dirs, bands, wide, high, deep), jnp.float32),
            jax.ShapeDtypeStruct((wide, high, deep), jnp.float32),
        ],
        scratch_shapes=[
            pltpu.VMEM((groups, local_dirs, wide, high, deep), jnp.float32),
            dma((2 * groups + 1,)),
        ],
        compiler_params=pltpu.CompilerParams(vmem_limit_bytes=4 << 20),
    )(*parts)


def beam_coeffs(abs_speed):
    return (
        1.0 - 1.5 * abs_speed + 0.5 * abs_speed * abs_speed,
        2.0 * abs_speed - abs_speed * abs_speed,
        0.5 * abs_speed * abs_speed - 0.5 * abs_speed,
    )


def on_device(
    phonon_heat_density,
    directions,
    quad_weight,
    mirror,
    band_courant,
    relax_rate,
    mode_heat_magnitude,
    mode_pulsation,
    wall_blocks,
    wall_count,
    wall_facet,
):
    local_dirs, bands, wide, high, deep = phonon_heat_density.shape
    tiles, groups = lax.axis_size("space"), lax.axis_size("dir")
    share = -(-bands // groups)
    extra = share * groups - bands
    home = phonon_heat_density
    if extra:
        home = jnp.pad(home, ((0, 0), (0, extra), (0, 0), (0, 0), (0, 0)))
    scalars = (
        directions,
        quad_weight,
        band_courant,
        relax_rate,
        mode_heat_magnitude,
        mode_pulsation,
    )
    walls = (wall_blocks, wall_count, wall_facet)
    return steps(tiles, groups, share, scalars, walls, (directions, mirror), home)


def solution(mesh):
    in_specs = (
        P("dir", None, "space", None, None),
        P(),
        P(),
        P(),
        P(),
        P(),
        P(),
        P(),
        P("space", None),
        P("space"),
        P("space", None, None),
    )
    out_specs = (P("dir", None, "space", None, None), P("space", None, None))
    return jax.shard_map(
        on_device, mesh=mesh, in_specs=in_specs, out_specs=out_specs, check_vma=False
    )
```

```python
import functools

import jax
import jax.numpy as jnp
from jax import lax
from jax.experimental import pallas as pl
from jax.experimental.pallas import tpu as pltpu
from jax.sharding import PartitionSpec as P

NEWTON = 4
BLOCK = 128
OCT = 8


def flat(values, axis):
    return jnp.sum(values, axis=axis, keepdims=True)


def orbit_order(directions, mirror):
    count = directions.shape[1]
    lane = lax.broadcasted_iota(jnp.int32, (count, count), 1).astype(jnp.float32)
    line = lax.broadcasted_iota(jnp.int32, (count, count), 0).astype(jnp.float32)
    same = lane == line
    positive = [jnp.where(directions[a : a + 1] > 0, 1.0, 0.0) for a in range(3)]
    code = positive[0] + 2.0 * positive[1] + 4.0 * positive[2]
    rep = flat(jnp.where(same, lane, 0.0), 1)
    for a in range(3):
        partner = mirror[a : a + 1].astype(jnp.float32)
        flipped = flat(jnp.where(rep == lane, partner, 0.0), 1)
        ahead = flat(jnp.where(same, positive[a], 0.0), 1)
        rep = jnp.where(ahead > 0.5, rep, flipped)
    rank = flat(jnp.where(lane < rep, jnp.where(code == OCT - 1, 1.0, 0.0), 0.0), 1)
    position = OCT * rank + flat(jnp.where(same, code, 0.0), 1)
    order = flat(jnp.where(position == lane, line, 0.0), 0)
    position = flat(jnp.where(same, position, 0.0), 0)
    return [jnp.clip(v.astype(jnp.int32), 0, count - 1) for v in (order, position)]


def facet_grid(blocks_ref, count_ref, wall_ref, rows, deep):
    cuts = deep // BLOCK
    row_id = lax.broadcasted_iota(jnp.int32, (rows, BLOCK), 0)
    grid = []
    for h in range(cuts):
        facets = jnp.zeros((rows, BLOCK), jnp.int32)
        for slot in range(wall_ref.shape[1]):
            block = jnp.where(slot < count_ref[0], blocks_ref[0, slot], -1)
            facets = jnp.where(
                row_id * cuts + h == block, wall_ref[0, slot : slot + 1, :], facets
            )
        grid.append(facets.astype(jnp.float32))
    return grid


def roll(u, by, axis):
    return pltpu.roll(u, by % u.shape[axis], axis)


def unit_coeffs(scalars, band, orbit):
    order_ref, directions_ref, weight_ref, courant_ref, rate_ref = scalars
    bands = courant_ref.shape[0]
    real = band < bands
    index = jnp.minimum(band, bands - 1)
    courant, rate = courant_ref[index], jnp.where(real, rate_ref[index], 0.0)
    rep = order_ref[0, orbit * OCT + OCT - 1]
    coef = []
    for axis_num in range(3):
        coef.extend(beam_coeffs(courant * jnp.abs(directions_ref[axis_num, rep])))
    coef.append(rate * weight_ref[rep])
    return coef, rate


def surplus_of(q):
    series = jnp.ones_like(q)
    for n in range(9, 1, -1):
        series = 1.0 + series * (q * (1.0 / n))
    return jnp.where(q < 0.5, q * series, jnp.exp(q) - 1.0)


def newton(rate_ref, magnitude_ref, pulsation_ref, source):
    kelvin = jnp.ones_like(source)
    for newton_turn in range(NEWTON):
        inverse = 1.0 / kelvin

        def one(b, carry):
            mismatch, gradient = carry
            factor = rate_ref[b] * magnitude_ref[b]
            q = pulsation_ref[b] * inverse
            surplus = surplus_of(q)
            ratio = 1.0 / surplus
            term = factor * ratio
            return mismatch + term, gradient + term * q * ((surplus + 1.0) * ratio)

        zero = jnp.zeros_like(source)
        mismatch, gradient = lax.fori_loop(0, rate_ref.shape[0], one, (zero, zero), unroll=8)
        mismatch, gradient = mismatch - source, gradient * inverse
        kelvin = jnp.clip(kelvin - mismatch / gradient, 0.5 * kelvin, 2.0 * kelvin)
    return kelvin


def sweep_unit(high, tiles, coef, facets_ref, load, store):
    _, rows, width = facets_ref.shape
    row_id = lax.broadcasted_iota(jnp.int32, (rows, width), 0)
    height = row_id % high
    total = [jnp.zeros((rows, width), jnp.float32) for _ in range(tiles)]
    for o in range(OCT):
        way = [1 if o >> a & 1 else -1 for a in range(3)]
        cells = []
        for t in range(tiles):
            facets = facets_ref[t]
            u = load(t, o)
            for a in range(3):
                facing = float(2 * a + 1 if way[a] > 0 else 2 * a + 2)
                u = jnp.where(facets == facing, load(t, o ^ (1 << a)), u)
            cells.append(u)
        turned = [roll(u, high * way[0], 0) for u in cells]
        for t in range(tiles):
            up = (t - way[0]) % tiles
            edge = row_id < high if way[0] > 0 else row_id >= rows - high
            near = jnp.where(edge, turned[up], turned[t])
            u = coef[0] * cells[t] + coef[1] * near + coef[2] * cells[up]
            u = coef[3] * u + coef[4] * roll(u, way[1], 1) + coef[5] * roll(u, 2 * way[1], 1)
            wrap1 = height < 1 if way[2] > 0 else height >= high - 1
            wrap2 = height < 2 if way[2] > 0 else height >= high - 2
            near = jnp.where(wrap1, roll(u, (1 - high) * way[2], 0), roll(u, way[2], 0))
            far = jnp.where(wrap2, roll(u, (2 - high) * way[2], 0), roll(u, 2 * way[2], 0))
            u = coef[6] * u + coef[7] * near + coef[8] * far
            store(t, o, u)
            total[t] = total[t] + u
    return [coef[9] * total[t] for t in range(tiles)]


MESH = pl.DeviceIdType.MESH


def greet(tile, tiles, group, groups, halves):
    barrier = pltpu.get_barrier_semaphore()
    peers = [(lax.rem(tile + u, tiles), group) for u in range(1, tiles)]
    peers += [(tile, lax.rem(group + t, groups)) for t in range(1, groups)]
    if halves > 1:
        peers += [(lax.rem(tile + u, tiles), lax.bitwise_xor(group, 1)) for u in range(1, tiles)]
    for peer in peers:
        pl.semaphore_signal(barrier, inc=1, device_id=peer, device_id_type=MESH)
    return barrier, len(peers)


def remote(src, dst, send, recv, device):
    return pltpu.make_async_remote_copy(
        src_ref=src, dst_ref=dst, send_sem=send, recv_sem=recv, device_id=device, device_id_type=MESH
    )


WAYS = (1, 2, -1, -2)
UNROLL = 8


def steps_kernel(
    tiles, groups, small, *refs
):
    given, (home_ref, out_ref, home_back, kelvin_ref) = refs[:small], refs[small : small + 4]
    held, scratch = refs[small + 4 : 2 * small + 4], refs[2 * small + 4 : -1]
    (
        directions_ref, weight_ref, courant_ref, rate_ref, magnitude_ref, pulsation_ref, blocks_ref,
        count_ref, vectors_ref, mirror_ref, wall_ref,
    ) = held
    inputs = [
        pltpu.make_async_copy(src, dst, refs[-1].at[n])
        for n, (src, dst) in enumerate(zip(given, held))
    ]
    local_dirs, slots, wide, high, deep = home_ref.shape
    share, rows, bands = slots // groups, wide * high, courant_ref.shape[0]
    dirs = local_dirs * groups
    part = dirs // tiles
    orbits = part // OCT
    landed, sorted_refs, fields, swept, back, unsorted = (
        scratch[n * share : (n + 1) * share] for n in range(6)
    )
    (
        order_ref, position_ref, ids_ref, facet_ref, coef_ref, between, facets_ref, source_ref, near, summed, near_half,
        partial_ref, far, found, given_half, shared, kelvins,
        dir_send, dir_recv, tile_send, tile_recv, rev_send, rev_recv, ret_send, ret_recv,
        facet_send, facet_recv, near_send, near_recv, pair_send, pair_recv, far_send, far_recv, last_send, last_recv, own_sem,
    ) = scratch[6 * share :]
    scalars = (order_ref, directions_ref, weight_ref, courant_ref, rate_ref)
    tile, group = lax.axis_index("space"), lax.axis_index("dir")

    halves = summed.shape[1]
    half = deep // halves
    mine = lax.rem(group, halves)
    mate = (tile, lax.bitwise_xor(group, 1))
    lanes = [slice(h * half, (h + 1) * half) for h in range(halves)]

    def to_tiles(u):
        return (lax.rem(tile + u, tiles), group)

    def other(t):
        if groups & (groups - 1):
            return lax.rem(group + t, groups)
        return lax.bitwise_xor(group, t)

    def sender(t):
        if groups & (groups - 1):
            return lax.rem(group + groups - t, groups)
        return lax.bitwise_xor(group, t)

    def to_groups(t):
        return (tile, other(t))

    own = [
        pltpu.make_async_copy(
            home_ref.at[:, group * share + k],
            landed[k].at[pl.ds(group * local_dirs, local_dirs)],
            own_sem.at[0, k],
        )
        for k in range(share)
    ]
    barrier, greeted = greet(tile, tiles, group, groups, halves)
    for copy in own + inputs:
        copy.start()
    pl.semaphore_wait(barrier, greeted)

    first = []
    for k in range(share):
        line = []
        for t in range(1, groups):
            peer = other(t)
            copy = remote(
                home_ref.at[:, peer * share + k],
                landed[k].at[pl.ds(group * local_dirs, local_dirs)],
                dir_send.at[k, t],
                dir_recv.at[k, t],
                to_groups(t),
            )
            copy.start()
            line.append(copy)
        first.append(line)

    for copy in inputs:
        copy.wait()
    order, position = orbit_order(vectors_ref[...], mirror_ref[...])
    ids_ref[0] = order
    ids_ref[1] = position
    tables = [
        pltpu.make_async_copy(ids_ref.at[0], order_ref, own_sem.at[5, 0]),
        pltpu.make_async_copy(ids_ref.at[1], position_ref, own_sem.at[6, 0]),
    ]
    for copy in tables:
        copy.start()
    for h, facets in enumerate(facet_grid(blocks_ref, count_ref, wall_ref, rows, deep)):
        facet_ref[:, h * BLOCK : (h + 1) * BLOCK] = facets
    own_facets = pltpu.make_async_copy(facet_ref, facets_ref.at[tile], own_sem.at[4, 0])
    own_facets.start()
    third = []
    for u in range(1, tiles):
        copy = remote(
            facet_ref, facets_ref.at[tile], facet_send.at[u], facet_recv.at[u], to_tiles(u)
        )
        copy.start()
        third.append(copy)
    source_ref[...] = jnp.zeros_like(source_ref)

    second, fourth, fifth = [], [], []
    turns = sorted(set(n % high for n in WAYS) - {0})
    width = 12 + len(turns)

    def table(b, carry):
        def one(d, carry):
            index, base = group * local_dirs + d, (b * local_dirs + d) * width
            line = []
            for a in range(3):
                line.append(both_ways(courant_ref[b] * directions_ref[a, index]))
            cz = [line[2][0]] + [0.0] * len(turns)
            for n, c in zip(WAYS, line[2][1:]):
                at = turns.index(n % high) + 1 if n % high else 0
                cz[at] = cz[at] + c
            values = list(line[0]) + list(line[1]) + cz
            values.append(rate_ref[b] * rate_ref[b] * weight_ref[index])
            for n, value in enumerate(values):
                coef_ref[base + n] = value
            return carry

        return lax.fori_loop(0, local_dirs, one, carry)

    lax.fori_loop(0, bands, table, 0)
    for copy in tables:
        copy.wait()

    last, early = share - 1, max(share - 3, 0)

    def gather(k):
        own[k].wait()
        for copy in first[k]:
            copy.wait_recv()

        def move(j, carry):
            d = order_ref[0, j]
            for x in range(wide):
                sorted_refs[k][j, x * high : (x + 1) * high, :] = landed[k][d, x]
            return carry

        lax.fori_loop(0, dirs, move, 0, unroll=16)
        line = [
            pltpu.make_async_copy(
                sorted_refs[k].at[pl.ds(tile * part, part)], fields[k].at[tile], own_sem.at[1, k]
            )
        ]
        for u in range(1, tiles):
            peer = lax.rem(tile + u, tiles)
            line.append(
                remote(
                    sorted_refs[k].at[pl.ds(peer * part, part)],
                    fields[k].at[tile],
                    tile_send.at[k, u],
                    tile_recv.at[k, u],
                    to_tiles(u),
                )
            )
        for copy in line:
            copy.start()
        second.append(line)

    def first_half(k, orbit, keep):
        coef, _ = unit_coeffs(scalars, group * share + k, tile * orbits + orbit)
        sums = sweep_unit(
            high, tiles, coef, facets_ref, lambda t, o: fields[k][t, orbit * OCT + o], keep
        )
        for t in range(tiles):
            source_ref[0, t] = source_ref[0, t] + sums[t]

    def second_half(k, orbit, load, result):
        coef, rate = unit_coeffs(scalars, group * share + k, tile * orbits + orbit)
        left = 1.0 - rate
        coef = coef[:6] + [left * c for c in coef[6:9]] + coef[9:]

        def keep(t, o, u):
            result[t, orbit * OCT + o] = left * u

        sums = sweep_unit(high, tiles, coef, facets_ref, load, keep)
        for t in range(tiles):
            source_ref[1, t] = source_ref[1, t] + sums[t]

    def arrive(k):
        second[k][0].wait()
        for copy in second[k][1:]:
            copy.wait_recv()

    def sweep(k):
        arrive(k)

        def one(orbit, carry):
            def keep(t, o, u):
                between[t, o] = u

            first_half(k, orbit, keep)
            second_half(k, orbit, lambda t, o: between[t, o], swept[k])
            return carry

        lax.fori_loop(0, orbits, one, 0)

    def sweep_first(k):
        arrive(k)

        def one(orbit, carry):
            def keep(t, o, u):
                swept[k][t, orbit * OCT + o] = u

            first_half(k, orbit, keep)
            return carry

        lax.fori_loop(0, orbits, one, 0)

    def sweep_second(k):
        def one(orbit, carry):
            second_half(k, orbit, lambda t, o: swept[k][t, orbit * OCT + o], fields[k])
            return carry

        lax.fori_loop(0, orbits, one, 0)

    def turn(k):
        done = fields[k] if k == last else swept[k]
        line = [
            pltpu.make_async_copy(
                done.at[tile], back[k].at[pl.ds(tile * part, part)], own_sem.at[2, k]
            )
        ]
        for u in range(1, tiles):
            peer = lax.rem(tile + u, tiles)
            line.append(
                remote(
                    done.at[peer],
                    back[k].at[pl.ds(tile * part, part)],
                    rev_send.at[k, u],
                    rev_recv.at[k, u],
                    to_tiles(u),
                )
            )
        for copy in line:
            copy.start()
        fourth.append(line)

    def scatter(k):
        fourth[k][0].wait()
        for copy in fourth[k][1:]:
            copy.wait_recv()

        def move(d, carry):
            j = position_ref[0, d]
            for x in range(wide):
                unsorted[k][d, x] = back[k][j, x * high : (x + 1) * high, :]
            return carry

        lax.fori_loop(0, dirs, move, 0, unroll=16)

    def send_home(k):
        line = [
            pltpu.make_async_copy(
                unsorted[k].at[pl.ds(group * local_dirs, local_dirs)],
                home_back.at[:, group * share + k],
                own_sem.at[3, k],
            )
        ]
        for t in range(1, groups):
            peer = other(t)
            line.append(
                remote(
                    unsorted[k].at[pl.ds(peer * local_dirs, local_dirs)],
                    home_back.at[:, group * share + k],
                    ret_send.at[k, t],
                    ret_recv.at[k, t],
                    to_groups(t),
                )
            )
        for copy in line:
            copy.start()
        fifth.append(line)

    def sum_groups(n):
        value, copies = summed[n, mine], []
        if halves > 1:
            copy = remote(
                summed.at[n, 1 - mine], near_half.at[n], pair_send.at[n], pair_recv.at[n], mate
            )
            copy.start()
            copy.wait_recv()
            value = value + near_half[n]
            copies.append(copy)
        partial_ref[n] = value
        place = group // halves
        fars = []
        for t in range(1, groups // halves):
            fars.append(
                remote(
                    partial_ref.at[n],
                    far.at[n, place],
                    far_send.at[n, t],
                    far_recv.at[n, t],
                    to_groups(t * halves),
                )
            )
        for copy in fars:
            copy.start()
        far[n, place] = value
        return copies, fars

    def total_of(n, copies):
        for copy in copies:
            copy.wait_recv()
        value = far[n, 0]
        for g in range(1, groups // halves):
            value = value + far[n, g]
        return newton(rate_ref, magnitude_ref, pulsation_ref, value)

    for k in range(share):
        if k > 0:
            sweep(k - 1)
            if k - 1 < early:
                turn(k - 1)
        gather(k)
        if k == 0:
            own_facets.wait()
            for copy in third:
                copy.wait_recv()
        if 2 <= k < early + 2:
            scatter(k - 2)
            send_home(k - 2)
    def sum_tiles(n):
        copies = []
        for u in range(1, tiles):
            peer = lax.rem(tile + u, tiles)
            copy = remote(
                source_ref.at[n, peer],
                near.at[u, n],
                near_send.at[n, u],
                near_recv.at[n, u],
                to_tiles(u),
            )
            copy.start()
            copies.append(copy)
        return copies

    def sum_of(n, copies):
        value = source_ref[n, tile]
        for u in range(1, tiles):
            copies[u - 1].wait_recv()
            value = value + near[u, n]
        return value

    sweep_first(last)
    nears = sum_tiles(0)
    for k in range(early, last):
        turn(k)
    sweep_second(last)
    value = sum_of(0, nears)
    for h in range(halves):
        summed[0, h] = value[:, lanes[h]]
    pairs, fars = sum_groups(0)
    while len(fifth) < share - 1:
        scatter(len(fifth))
        send_home(len(fifth))
    value = total_of(0, fars)
    shared[...] = value
    lasts = []
    for u in range(tiles):
        for m in range(halves):
            if u or m:
                target = (lax.rem(tile + u, tiles), lax.bitwise_xor(group, m))
                n = u * halves + m
                copy = remote(
                    shared, kelvins.at[tile, mine], last_send.at[n], last_recv.at[n], target
                )
                copy.start()
                lasts.append(copy)
    kelvins[tile, mine] = value
    last_nears = sum_tiles(1)
    turn(last)
    for copy in lasts:
        copy.wait_recv()

    below, above = lax.rem(tile + tiles - 1, tiles), lax.rem(tile + 1, tiles)
    row_id = lax.broadcasted_iota(jnp.int32, (rows, deep), 0)
    height = row_id % high

    def spin(u, n):
        return jnp.where(height < n, roll(u, n - high, 0), roll(u, n, 0))

    def drift_coeffs(d, b):
        base = (b * local_dirs + d) * width
        values = [coef_ref[base + n] for n in range(width)]
        return values[:5], values[5:10], values[10:-1], values[-1]

    def drift(b, acc):
        left = (1.0 - rate_ref[b]) * rate_ref[b]

        def bose(t):
            warm = jnp.concatenate([kelvins[t, h] for h in range(halves)], axis=1)
            return magnitude_ref[b] / surplus_of(pulsation_ref[b] / warm)

        here, low, up = bose(tile), bose(below), bose(above)
        shifted = [
            here,
            jnp.where(row_id < high, roll(low, high, 0), roll(here, high, 0)),
            low,
            jnp.where(row_id >= rows - high, roll(up, -high, 0), roll(here, -high, 0)),
            up,
        ]

        def one(d, acc):
            cx, cy, cz, weight = drift_coeffs(d, b)
            u = combine(cx, shifted)
            u = combine(cy, [u] + [roll(u, n, 1) for n in WAYS])
            u = combine(cz, [u] + [spin(u, n) for n in turns])
            kept = left * u
            for x in range(wide):
                out_ref[d, b, x] = kept[x * high : (x + 1) * high]
            return acc + weight * u

        return lax.fori_loop(0, local_dirs, one, acc, unroll=UNROLL)

    acc = lax.fori_loop(0, bands, drift, jnp.zeros((rows, deep), jnp.float32))
    value = sum_of(1, last_nears) + acc
    for h in range(halves):
        summed[1, h] = value[:, lanes[h]]
    pair, last_fars = sum_groups(1)
    scatter(last)
    send_home(last)
    value = total_of(1, last_fars)
    found[mine] = value
    if halves > 1:
        given_half[...] = value
        copy = remote(given_half, found.at[mine], pair_send.at[2], pair_recv.at[2], mate)
        copy.start()
        copy.wait_recv()
        pair.append(copy)
    for h in range(halves):
        value = found[h]
        for x in range(wide):
            kelvin_ref[x, :, lanes[h]] = value[x * high : (x + 1) * high]
    fars = pairs + fars + pair + last_fars + last_nears

    def settle(b, carry):
        warm = jnp.concatenate([found[h] for h in range(halves)], axis=1)
        heat = rate_ref[b] * (magnitude_ref[b] / surplus_of(pulsation_ref[b] / warm))

        def one(d, carry):
            for x in range(wide):
                out_ref[d, b, x] = out_ref[d, b, x] + heat[x * high : (x + 1) * high]
            return carry

        return lax.fori_loop(0, local_dirs, one, carry, unroll=4)

    lax.fori_loop(0, bands, settle, 0)
    for k in range(share):
        for t in range(groups):
            if t:
                fifth[k][t].wait_recv()
            else:
                fifth[k][0].wait()
            if k == last:
                continue
            b = sender(t) * share + k

            def one(d, carry):
                for x in range(wide):
                    out_ref[d, b, x] = out_ref[d, b, x] + home_back[d, b, x]
                return carry

            if share * groups == bands:
                lax.fori_loop(0, local_dirs, one, 0, unroll=8)
            else:
                lax.fori_loop(0, jnp.where(b < bands, local_dirs, 0), one, 0)
    for copy in third + nears + fars + lasts:
        copy.wait_send()
    for line in first:
        for copy in line:
            copy.wait_send()
    for line in second + fourth + fifth:
        for copy in line[1:]:
            copy.wait_send()


def settle_kernel(groups, sum_ref, home_back, kelvin_ref, out_ref, kelvin_out, last_ref, sems):
    local_dirs, bands, wide = sum_ref.shape[:3]
    share = home_back.shape[1] // groups
    copies = [pltpu.make_async_copy(kelvin_ref, kelvin_out, sems.at[2 * groups])]
    for g in range(groups):
        count = min(bands - g * share, share - 1)
        if count > 0:
            part = pl.ds(g * share, count)
            copies.append(
                pltpu.make_async_copy(sum_ref.at[:, part], out_ref.at[:, part], sems.at[g])
            )
    for copy in copies:
        copy.start()
    for g in range(groups):
        b = (g + 1) * share - 1
        if b < bands:

            def one(d, carry):
                for x in range(wide):
                    last_ref[g, d, x] = sum_ref[d, b, x] + home_back[d, b, x]
                return carry

            lax.fori_loop(0, local_dirs, one, 0, unroll=8)
            copy = pltpu.make_async_copy(last_ref.at[g], out_ref.at[:, b], sems.at[groups + g])
            copy.start()
            copies.append(copy)
    for copy in copies:
        copy.wait()


def both_ways(speed):
    centre, near, far = beam_coeffs(jnp.abs(speed))
    forward = speed > 0
    return (
        centre,
        jnp.where(forward, near, 0.0),
        jnp.where(forward, far, 0.0),
        jnp.where(forward, 0.0, near),
        jnp.where(forward, 0.0, far),
    )


def combine(coef, moves):
    total = coef[0] * moves[0]
    for c, move in zip(coef[1:], moves[1:]):
        total = total + c * move
    return total


def steps(tiles, groups, share, scalars, walls, vectors, home):
    local_dirs, _, wide, high, deep = home.shape
    dirs, rows = local_dirs * groups, wide * high
    part = dirs // tiles
    bands = scalars[2].shape[0]
    halves = 2 if groups % 2 == 0 and deep % (2 * BLOCK) == 0 else 1
    half = deep // halves
    vmem = pl.BlockSpec(memory_space=pltpu.VMEM)
    anywhere = pl.BlockSpec(memory_space=pl.ANY)
    dma = pltpu.SemaphoreType.DMA
    scratch = (
        [pltpu.VMEM((dirs, wide, high, deep), jnp.float32)] * share
        + [pltpu.VMEM((dirs, rows, deep), jnp.float32)] * share
        + [pltpu.VMEM((tiles, part, rows, deep), jnp.float32)] * (2 * share)
        + [pltpu.VMEM((dirs, rows, deep), jnp.float32)] * share
        + [pltpu.VMEM((dirs, wide, high, deep), jnp.float32)] * share
        + [
            pltpu.SMEM((1, dirs), jnp.int32),
            pltpu.SMEM((1, dirs), jnp.int32),
            pltpu.VMEM((2, 1, dirs), jnp.int32),
            pltpu.VMEM((rows, deep), jnp.float32),
            pltpu.SMEM((bands * local_dirs * (12 + len(set(n % high for n in WAYS) - {0})),), jnp.float32),
            pltpu.VMEM((tiles, OCT, rows, deep), jnp.float32),
            pltpu.VMEM((tiles, rows, deep), jnp.float32),
            pltpu.VMEM((2, tiles, rows, deep), jnp.float32),
            pltpu.VMEM((tiles, 2, rows, deep), jnp.float32),
            pltpu.VMEM((2, halves, rows, half), jnp.float32),
            pltpu.VMEM((2, rows, half), jnp.float32),
            pltpu.VMEM((2, rows, half), jnp.float32),
            pltpu.VMEM((2, groups // halves, rows, half), jnp.float32),
            pltpu.VMEM((halves, rows, half), jnp.float32),
            pltpu.VMEM((rows, half), jnp.float32),
            pltpu.VMEM((rows, half), jnp.float32),
            pltpu.VMEM((tiles, halves, rows, half), jnp.float32),
            dma((share, groups)),
            dma((share, groups)),
            dma((share, tiles)),
            dma((share, tiles)),
            dma((share, tiles)),
            dma((share, tiles)),
            dma((share, groups)),
            dma((share, groups)),
            dma((tiles,)),
            dma((tiles,)),
            dma((2, tiles)),
            dma((2, tiles)),
            dma((3,)),
            dma((3,)),
            dma((2, groups)),
            dma((2, groups)),
            dma((halves * tiles,)),
            dma((halves * tiles,)),
            dma((7, share)),
        ]
    )
    held = [pltpu.SMEM(v.shape, v.dtype) for v in (*scalars, *walls[:2])]
    held += [pltpu.VMEM(v.shape, v.dtype) for v in (*vectors, walls[2])]
    parts = pl.pallas_call(
        functools.partial(steps_kernel, tiles, groups, len(held)),
        in_specs=[anywhere] * (len(held) + 1),
        out_specs=[vmem] * 3,
        out_shape=[
            pltpu.VMEM((local_dirs, bands, wide, high, deep), jnp.float32),
            pltpu.VMEM((local_dirs, share * groups, wide, high, deep), jnp.float32),
            pltpu.VMEM((wide, high, deep), jnp.float32),
        ],
        scratch_shapes=held + scratch + [dma((len(held),))],
        compiler_params=pltpu.CompilerParams(
            collective_id=0, has_side_effects=True, vmem_limit_bytes=46 << 20
        ),
    )(*scalars, *walls[:2], *vectors, walls[2], home)
    return pl.pallas_call(
        functools.partial(settle_kernel, groups),
        in_specs=[vmem] * 3,
        out_specs=[anywhere] * 2,
        out_shape=[
            jax.ShapeDtypeStruct((local_dirs, bands, wide, high, deep), jnp.float32),
            jax.ShapeDtypeStruct((wide, high, deep), jnp.float32),
        ],
        scratch_shapes=[
            pltpu.VMEM((groups, local_dirs, wide, high, deep), jnp.float32),
            dma((2 * groups + 1,)),
        ],
        compiler_params=pltpu.CompilerParams(vmem_limit_bytes=4 << 20),
    )(*parts)


def beam_coeffs(abs_speed):
    return (
        1.0 - 1.5 * abs_speed + 0.5 * abs_speed * abs_speed,
        2.0 * abs_speed - abs_speed * abs_speed,
        0.5 * abs_speed * abs_speed - 0.5 * abs_speed,
    )


def on_device(
    phonon_heat_density,
    directions,
    quad_weight,
    mirror,
    band_courant,
    relax_rate,
    mode_heat_magnitude,
    mode_pulsation,
    wall_blocks,
    wall_count,
    wall_facet,
):
    local_dirs, bands, wide, high, deep = phonon_heat_density.shape
    tiles, groups = lax.axis_size("space"), lax.axis_size("dir")
    share = -(-bands // groups)
    extra = share * groups - bands
    home = phonon_heat_density
    if extra:
        home = jnp.pad(home, ((0, 0), (0, extra), (0, 0), (0, 0), (0, 0)))
    scalars = (
        directions,
        quad_weight,
        band_courant,
        relax_rate,
        mode_heat_magnitude,
        mode_pulsation,
    )
    walls = (wall_blocks, wall_count, wall_facet)
    return steps(tiles, groups, share, scalars, walls, (directions, mirror), home)


def solution(mesh):
    in_specs = (
        P("dir", None, "space", None, None),
        P(),
        P(),
        P(),
        P(),
        P(),
        P(),
        P(),
        P("space", None),
        P("space"),
        P("space", None, None),
    )
    out_specs = (P("dir", None, "space", None, None), P("space", None, None))
    return jax.shard_map(
        on_device, mesh=mesh, in_specs=in_specs, out_specs=out_specs, check_vma=False
    )
```

```python
import functools

import jax
import jax.numpy as jnp
from jax import lax
from jax.experimental import pallas as pl
from jax.experimental.pallas import tpu as pltpu
from jax.sharding import PartitionSpec as P

NEWTON = 4
BLOCK = 128
OCT = 8


def flat(values, axis):
    return jnp.sum(values, axis=axis, keepdims=True)


def orbit_order(directions, mirror):
    count = directions.shape[1]
    lane = lax.broadcasted_iota(jnp.int32, (count, count), 1).astype(jnp.float32)
    line = lax.broadcasted_iota(jnp.int32, (count, count), 0).astype(jnp.float32)
    same = lane == line
    positive = [jnp.where(directions[a : a + 1] > 0, 1.0, 0.0) for a in range(3)]
    code = positive[0] + 2.0 * positive[1] + 4.0 * positive[2]
    rep = flat(jnp.where(same, lane, 0.0), 1)
    for a in range(3):
        partner = mirror[a : a + 1].astype(jnp.float32)
        flipped = flat(jnp.where(rep == lane, partner, 0.0), 1)
        ahead = flat(jnp.where(same, positive[a], 0.0), 1)
        rep = jnp.where(ahead > 0.5, rep, flipped)
    rank = flat(jnp.where(lane < rep, jnp.where(code == OCT - 1, 1.0, 0.0), 0.0), 1)
    position = OCT * rank + flat(jnp.where(same, code, 0.0), 1)
    order = flat(jnp.where(position == lane, line, 0.0), 0)
    position = flat(jnp.where(same, position, 0.0), 0)
    return [jnp.clip(v.astype(jnp.int32), 0, count - 1) for v in (order, position)]


def facet_grid(blocks_ref, count_ref, wall_ref, rows, deep):
    cuts = deep // BLOCK
    row_id = lax.broadcasted_iota(jnp.int32, (rows, BLOCK), 0)
    grid = []
    for h in range(cuts):
        facets = jnp.zeros((rows, BLOCK), jnp.int32)
        for slot in range(wall_ref.shape[1]):
            block = jnp.where(slot < count_ref[0], blocks_ref[0, slot], -1)
            facets = jnp.where(
                row_id * cuts + h == block, wall_ref[0, slot : slot + 1, :], facets
            )
        grid.append(facets.astype(jnp.float32))
    return grid


def roll(u, by, axis):
    return pltpu.roll(u, by % u.shape[axis], axis)


def unit_coeffs(scalars, band, orbit):
    order_ref, directions_ref, weight_ref, courant_ref, rate_ref = scalars
    bands = courant_ref.shape[0]
    real = band < bands
    index = jnp.minimum(band, bands - 1)
    courant, rate = courant_ref[index], jnp.where(real, rate_ref[index], 0.0)
    rep = order_ref[0, orbit * OCT + OCT - 1]
    coef = []
    for axis_num in range(3):
        coef.extend(beam_coeffs(courant * jnp.abs(directions_ref[axis_num, rep])))
    coef.append(rate * weight_ref[rep])
    return coef, rate


def surplus_of(q):
    series = jnp.ones_like(q)
    for n in range(9, 1, -1):
        series = 1.0 + series * (q * (1.0 / n))
    return jnp.where(q < 0.5, q * series, jnp.exp(q) - 1.0)


def newton(rate_ref, magnitude_ref, pulsation_ref, source):
    kelvin = jnp.ones_like(source)
    for newton_turn in range(NEWTON):
        inverse = 1.0 / kelvin

        def one(b, carry):
            mismatch, gradient = carry
            factor = rate_ref[b] * magnitude_ref[b]
            q = pulsation_ref[b] * inverse
            surplus = surplus_of(q)
            ratio = 1.0 / surplus
            term = factor * ratio
            return mismatch + term, gradient + term * q * ((surplus + 1.0) * ratio)

        zero = jnp.zeros_like(source)
        mismatch, gradient = lax.fori_loop(0, rate_ref.shape[0], one, (zero, zero), unroll=8)
        mismatch, gradient = mismatch - source, gradient * inverse
        kelvin = jnp.clip(kelvin - mismatch / gradient, 0.5 * kelvin, 2.0 * kelvin)
    return kelvin


def sweep_unit(high, tiles, coef, facets_ref, load, store):
    _, rows, width = facets_ref.shape
    row_id = lax.broadcasted_iota(jnp.int32, (rows, width), 0)
    height = row_id % high
    total = [jnp.zeros((rows, width), jnp.float32) for _ in range(tiles)]
    for o in range(OCT):
        way = [1 if o >> a & 1 else -1 for a in range(3)]
        cells = []
        for t in range(tiles):
            facets = facets_ref[t]
            u = load(t, o)
            for a in range(3):
                facing = float(2 * a + 1 if way[a] > 0 else 2 * a + 2)
                u = jnp.where(facets == facing, load(t, o ^ (1 << a)), u)
            cells.append(u)
        turned = [roll(u, high * way[0], 0) for u in cells]
        for t in range(tiles):
            up = (t - way[0]) % tiles
            edge = row_id < high if way[0] > 0 else row_id >= rows - high
            near = jnp.where(edge, turned[up], turned[t])
            u = coef[0] * cells[t] + coef[1] * near + coef[2] * cells[up]
            u = coef[3] * u + coef[4] * roll(u, way[1], 1) + coef[5] * roll(u, 2 * way[1], 1)
            wrap1 = height < 1 if way[2] > 0 else height >= high - 1
            wrap2 = height < 2 if way[2] > 0 else height >= high - 2
            near = jnp.where(wrap1, roll(u, (1 - high) * way[2], 0), roll(u, way[2], 0))
            far = jnp.where(wrap2, roll(u, (2 - high) * way[2], 0), roll(u, 2 * way[2], 0))
            u = coef[6] * u + coef[7] * near + coef[8] * far
            store(t, o, u)
            total[t] = total[t] + u
    return [coef[9] * total[t] for t in range(tiles)]


MESH = pl.DeviceIdType.MESH


def greet(tile, tiles, group, groups, halves):
    barrier = pltpu.get_barrier_semaphore()
    peers = [(lax.rem(tile + u, tiles), group) for u in range(1, tiles)]
    peers += [(tile, lax.rem(group + t, groups)) for t in range(1, groups)]
    if halves > 1:
        peers += [(lax.rem(tile + u, tiles), lax.bitwise_xor(group, 1)) for u in range(1, tiles)]
    for peer in peers:
        pl.semaphore_signal(barrier, inc=1, device_id=peer, device_id_type=MESH)
    return barrier, len(peers)


def remote(src, dst, send, recv, device):
    return pltpu.make_async_remote_copy(
        src_ref=src, dst_ref=dst, send_sem=send, recv_sem=recv, device_id=device, device_id_type=MESH
    )


WAYS = (1, 2, -1, -2)
UNROLL = 8


def steps_kernel(
    tiles, groups, small, *refs
):
    given, (home_ref, out_ref, home_back, kelvin_ref) = refs[:small], refs[small : small + 4]
    held, scratch = refs[small + 4 : 2 * small + 4], refs[2 * small + 4 : -1]
    (
        directions_ref, weight_ref, courant_ref, rate_ref, magnitude_ref, pulsation_ref, blocks_ref,
        count_ref, vectors_ref, mirror_ref, wall_ref,
    ) = held
    inputs = [
        pltpu.make_async_copy(src, dst, refs[-1].at[n])
        for n, (src, dst) in enumerate(zip(given, held))
    ]
    local_dirs, slots, wide, high, deep = home_ref.shape
    share, rows, bands = slots // groups, wide * high, courant_ref.shape[0]
    dirs = local_dirs * groups
    part = dirs // tiles
    orbits = part // OCT
    landed, sorted_refs, fields, swept, back, unsorted = (
        scratch[n * share : (n + 1) * share] for n in range(6)
    )
    (
        order_ref, position_ref, ids_ref, facet_ref, coef_ref, between, facets_ref, source_ref, near, summed, near_half,
        partial_ref, far, found, given_half, shared, kelvins,
        dir_send, dir_recv, tile_send, tile_recv, rev_send, rev_recv, ret_send, ret_recv,
        facet_send, facet_recv, near_send, near_recv, pair_send, pair_recv, far_send, far_recv, last_send, last_recv, own_sem,
    ) = scratch[6 * share :]
    scalars = (order_ref, directions_ref, weight_ref, courant_ref, rate_ref)
    tile, group = lax.axis_index("space"), lax.axis_index("dir")

    halves = summed.shape[1]
    half = deep // halves
    mine = lax.rem(group, halves)
    mate = (tile, lax.bitwise_xor(group, 1))
    lanes = [slice(h * half, (h + 1) * half) for h in range(halves)]

    def to_tiles(u):
        return (lax.rem(tile + u, tiles), group)

    def other(t):
        if groups & (groups - 1):
            return lax.rem(group + t, groups)
        return lax.bitwise_xor(group, t)

    visits = list(range(1, groups))
    if groups % 2 == 0:
        visits = visits[:1] + [t ^ 1 for t in visits[1:]]

    def sender(t):
        if groups & (groups - 1):
            return lax.rem(group + groups - t, groups)
        return lax.bitwise_xor(group, t)

    def to_groups(t):
        return (tile, other(t))

    own = [
        pltpu.make_async_copy(
            home_ref.at[:, group * share + k],
            landed[k].at[pl.ds(group * local_dirs, local_dirs)],
            own_sem.at[0, k],
        )
        for k in range(share)
    ]
    barrier, greeted = greet(tile, tiles, group, groups, halves)
    for copy in own + inputs:
        copy.start()
    pl.semaphore_wait(barrier, greeted)

    first = []
    for k in range(share):
        line = []
        for t in visits:
            peer = other(t)
            copy = remote(
                home_ref.at[:, peer * share + k],
                landed[k].at[pl.ds(group * local_dirs, local_dirs)],
                dir_send.at[k, t],
                dir_recv.at[k, t],
                to_groups(t),
            )
            copy.start()
            line.append(copy)
        first.append(line)

    for copy in inputs:
        copy.wait()
    order, position = orbit_order(vectors_ref[...], mirror_ref[...])
    ids_ref[0] = order
    ids_ref[1] = position
    tables = [
        pltpu.make_async_copy(ids_ref.at[0], order_ref, own_sem.at[5, 0]),
        pltpu.make_async_copy(ids_ref.at[1], position_ref, own_sem.at[6, 0]),
    ]
    for copy in tables:
        copy.start()
    for h, facets in enumerate(facet_grid(blocks_ref, count_ref, wall_ref, rows, deep)):
        facet_ref[:, h * BLOCK : (h + 1) * BLOCK] = facets
    own_facets = pltpu.make_async_copy(facet_ref, facets_ref.at[tile], own_sem.at[4, 0])
    own_facets.start()
    third = []
    for u in range(1, tiles):
        copy = remote(
            facet_ref, facets_ref.at[tile], facet_send.at[u], facet_recv.at[u], to_tiles(u)
        )
        copy.start()
        third.append(copy)
    source_ref[...] = jnp.zeros_like(source_ref)

    second, fourth, fifth = [], [], []
    turns = sorted(set(n % high for n in WAYS) - {0})
    width = 12 + len(turns)

    def table(b, carry):
        def one(d, carry):
            index, base = group * local_dirs + d, (b * local_dirs + d) * width
            line = []
            for a in range(3):
                line.append(both_ways(courant_ref[b] * directions_ref[a, index]))
            cz = [line[2][0]] + [0.0] * len(turns)
            for n, c in zip(WAYS, line[2][1:]):
                at = turns.index(n % high) + 1 if n % high else 0
                cz[at] = cz[at] + c
            values = list(line[0]) + list(line[1]) + cz
            values.append(rate_ref[b] * rate_ref[b] * weight_ref[index])
            for n, value in enumerate(values):
                coef_ref[base + n] = value
            return carry

        return lax.fori_loop(0, local_dirs, one, carry)

    lax.fori_loop(0, bands, table, 0)
    for copy in tables:
        copy.wait()

    last, early = share - 1, max(share - 3, 0)

    def gather(k):
        own[k].wait()
        for copy in first[k]:
            copy.wait_recv()

        def move(j, carry):
            d = order_ref[0, j]
            for x in range(wide):
                sorted_refs[k][j, x * high : (x + 1) * high, :] = landed[k][d, x]
            return carry

        lax.fori_loop(0, dirs, move, 0, unroll=16)
        line = [
            pltpu.make_async_copy(
                sorted_refs[k].at[pl.ds(tile * part, part)], fields[k].at[tile], own_sem.at[1, k]
            )
        ]
        for u in range(1, tiles):
            peer = lax.rem(tile + u, tiles)
            line.append(
                remote(
                    sorted_refs[k].at[pl.ds(peer * part, part)],
                    fields[k].at[tile],
                    tile_send.at[k, u],
                    tile_recv.at[k, u],
                    to_tiles(u),
                )
            )
        for copy in line:
            copy.start()
        second.append(line)

    def first_half(k, orbit, keep):
        coef, _ = unit_coeffs(scalars, group * share + k, tile * orbits + orbit)
        sums = sweep_unit(
            high, tiles, coef, facets_ref, lambda t, o: fields[k][t, orbit * OCT + o], keep
        )
        for t in range(tiles):
            source_ref[0, t] = source_ref[0, t] + sums[t]

    def second_half(k, orbit, load, result):
        coef, rate = unit_coeffs(scalars, group * share + k, tile * orbits + orbit)
        left = 1.0 - rate
        coef = coef[:6] + [left * c for c in coef[6:9]] + coef[9:]

        def keep(t, o, u):
            result[t, orbit * OCT + o] = left * u

        sums = sweep_unit(high, tiles, coef, facets_ref, load, keep)
        for t in range(tiles):
            source_ref[1, t] = source_ref[1, t] + sums[t]

    def arrive(k):
        second[k][0].wait()
        for copy in second[k][1:]:
            copy.wait_recv()

    def sweep(k):
        arrive(k)

        def one(orbit, carry):
            def keep(t, o, u):
                between[t, o] = u

            first_half(k, orbit, keep)
            second_half(k, orbit, lambda t, o: between[t, o], swept[k])
            return carry

        lax.fori_loop(0, orbits, one, 0)

    def sweep_first(k):
        arrive(k)

        def one(orbit, carry):
            def keep(t, o, u):
                swept[k][t, orbit * OCT + o] = u

            first_half(k, orbit, keep)
            return carry

        lax.fori_loop(0, orbits, one, 0)

    def sweep_second(k):
        def one(orbit, carry):
            second_half(k, orbit, lambda t, o: swept[k][t, orbit * OCT + o], fields[k])
            return carry

        lax.fori_loop(0, orbits, one, 0)

    def turn(k):
        done = fields[k] if k == last else swept[k]
        line = [
            pltpu.make_async_copy(
                done.at[tile], back[k].at[pl.ds(tile * part, part)], own_sem.at[2, k]
            )
        ]
        for u in range(1, tiles):
            peer = lax.rem(tile + u, tiles)
            line.append(
                remote(
                    done.at[peer],
                    back[k].at[pl.ds(tile * part, part)],
                    rev_send.at[k, u],
                    rev_recv.at[k, u],
                    to_tiles(u),
                )
            )
        for copy in line:
            copy.start()
        fourth.append(line)

    def scatter(k):
        fourth[k][0].wait()
        for copy in fourth[k][1:]:
            copy.wait_recv()

        def move(d, carry):
            j = position_ref[0, d]
            for x in range(wide):
                unsorted[k][d, x] = back[k][j, x * high : (x + 1) * high, :]
            return carry

        lax.fori_loop(0, dirs, move, 0, unroll=16)

    def send_home(k):
        line = [
            pltpu.make_async_copy(
                unsorted[k].at[pl.ds(group * local_dirs, local_dirs)],
                home_back.at[:, group * share + k],
                own_sem.at[3, k],
            )
        ]
        for t in visits:
            peer = other(t)
            line.append(
                remote(
                    unsorted[k].at[pl.ds(peer * local_dirs, local_dirs)],
                    home_back.at[:, group * share + k],
                    ret_send.at[k, t],
                    ret_recv.at[k, t],
                    to_groups(t),
                )
            )
        for copy in line:
            copy.start()
        fifth.append(line)

    def sum_groups(n):
        value, copies = summed[n, mine], []
        if halves > 1:
            copy = remote(
                summed.at[n, 1 - mine], near_half.at[n], pair_send.at[n], pair_recv.at[n], mate
            )
            copy.start()
            copy.wait_recv()
            value = value + near_half[n]
            copies.append(copy)
        partial_ref[n] = value
        place = group // halves
        fars = []
        for t in range(1, groups // halves):
            fars.append(
                remote(
                    partial_ref.at[n],
                    far.at[n, place],
                    far_send.at[n, t],
                    far_recv.at[n, t],
                    to_groups(t * halves),
                )
            )
        for copy in fars:
            copy.start()
        far[n, place] = value
        return copies, fars

    def total_of(n, copies):
        for copy in copies:
            copy.wait_recv()
        value = far[n, 0]
        for g in range(1, groups // halves):
            value = value + far[n, g]
        return newton(rate_ref, magnitude_ref, pulsation_ref, value)

    for k in range(share):
        if k > 0:
            sweep(k - 1)
            if k - 1 < early:
                turn(k - 1)
        gather(k)
        if k == 0:
            own_facets.wait()
            for copy in third:
                copy.wait_recv()
        if 2 <= k < early + 2:
            scatter(k - 2)
            send_home(k - 2)
    def sum_tiles(n):
        copies = []
        for u in range(1, tiles):
            peer = lax.rem(tile + u, tiles)
            copy = remote(
                source_ref.at[n, peer],
                near.at[u, n],
                near_send.at[n, u],
                near_recv.at[n, u],
                to_tiles(u),
            )
            copy.start()
            copies.append(copy)
        return copies

    def sum_of(n, copies):
        value = source_ref[n, tile]
        for u in range(1, tiles):
            copies[u - 1].wait_recv()
            value = value + near[u, n]
        return value

    sweep_first(last)
    nears = sum_tiles(0)
    for k in range(early, last):
        turn(k)
    sweep_second(last)
    value = sum_of(0, nears)
    for h in range(halves):
        summed[0, h] = value[:, lanes[h]]
    pairs, fars = sum_groups(0)
    while len(fifth) < share - 1:
        scatter(len(fifth))
        send_home(len(fifth))
    value = total_of(0, fars)
    shared[...] = value
    lasts = []
    for u in range(tiles):
        for m in range(halves):
            if u or m:
                target = (lax.rem(tile + u, tiles), lax.bitwise_xor(group, m))
                n = u * halves + m
                copy = remote(
                    shared, kelvins.at[tile, mine], last_send.at[n], last_recv.at[n], target
                )
                copy.start()
                lasts.append(copy)
    kelvins[tile, mine] = value
    last_nears = sum_tiles(1)
    turn(last)
    for copy in lasts:
        copy.wait_recv()

    below, above = lax.rem(tile + tiles - 1, tiles), lax.rem(tile + 1, tiles)
    row_id = lax.broadcasted_iota(jnp.int32, (rows, deep), 0)
    height = row_id % high

    def spin(u, n):
        return jnp.where(height < n, roll(u, n - high, 0), roll(u, n, 0))

    def drift_coeffs(d, b):
        base = (b * local_dirs + d) * width
        values = [coef_ref[base + n] for n in range(width)]
        return values[:5], values[5:10], values[10:-1], values[-1]

    def drift(b, acc):
        left = (1.0 - rate_ref[b]) * rate_ref[b]

        def bose(t):
            warm = jnp.concatenate([kelvins[t, h] for h in range(halves)], axis=1)
            return magnitude_ref[b] / surplus_of(pulsation_ref[b] / warm)

        here, low, up = bose(tile), bose(below), bose(above)
        shifted = [
            here,
            jnp.where(row_id < high, roll(low, high, 0), roll(here, high, 0)),
            low,
            jnp.where(row_id >= rows - high, roll(up, -high, 0), roll(here, -high, 0)),
            up,
        ]

        def one(d, acc):
            cx, cy, cz, weight = drift_coeffs(d, b)
            u = combine(cx, shifted)
            u = combine(cy, [u] + [roll(u, n, 1) for n in WAYS])
            u = combine(cz, [u] + [spin(u, n) for n in turns])
            kept = left * u
            for x in range(wide):
                out_ref[d, b, x] = kept[x * high : (x + 1) * high]
            return acc + weight * u

        return lax.fori_loop(0, local_dirs, one, acc, unroll=UNROLL)

    acc = lax.fori_loop(0, bands, drift, jnp.zeros((rows, deep), jnp.float32))
    value = sum_of(1, last_nears) + acc
    for h in range(halves):
        summed[1, h] = value[:, lanes[h]]
    pair, last_fars = sum_groups(1)
    scatter(last)
    send_home(last)
    value = total_of(1, last_fars)
    found[mine] = value
    if halves > 1:
        given_half[...] = value
        copy = remote(given_half, found.at[mine], pair_send.at[2], pair_recv.at[2], mate)
        copy.start()
        copy.wait_recv()
        pair.append(copy)
    for h in range(halves):
        value = found[h]
        for x in range(wide):
            kelvin_ref[x, :, lanes[h]] = value[x * high : (x + 1) * high]
    fars = pairs + fars + pair + last_fars + last_nears

    def settle(b, carry):
        warm = jnp.concatenate([found[h] for h in range(halves)], axis=1)
        heat = rate_ref[b] * (magnitude_ref[b] / surplus_of(pulsation_ref[b] / warm))

        def one(d, carry):
            for x in range(wide):
                out_ref[d, b, x] = out_ref[d, b, x] + heat[x * high : (x + 1) * high]
            return carry

        return lax.fori_loop(0, local_dirs, one, carry, unroll=4)

    lax.fori_loop(0, bands, settle, 0)
    for k in range(share):
        for n, t in enumerate([0] + visits):
            if n:
                fifth[k][n].wait_recv()
            else:
                fifth[k][0].wait()
            if k == last:
                continue
            b = sender(t) * share + k

            def one(d, carry):
                for x in range(wide):
                    out_ref[d, b, x] = out_ref[d, b, x] + home_back[d, b, x]
                return carry

            if share * groups == bands:
                lax.fori_loop(0, local_dirs, one, 0, unroll=8)
            else:
                lax.fori_loop(0, jnp.where(b < bands, local_dirs, 0), one, 0)
    for copy in third + nears + fars + lasts:
        copy.wait_send()
    for line in first:
        for copy in line:
            copy.wait_send()
    for line in second + fourth + fifth:
        for copy in line[1:]:
            copy.wait_send()


def settle_kernel(groups, sum_ref, home_back, kelvin_ref, out_ref, kelvin_out, last_ref, sems):
    local_dirs, bands, wide = sum_ref.shape[:3]
    share = home_back.shape[1] // groups
    copies = [pltpu.make_async_copy(kelvin_ref, kelvin_out, sems.at[2 * groups])]
    for g in range(groups):
        count = min(bands - g * share, share - 1)
        if count > 0:
            part = pl.ds(g * share, count)
            copies.append(
                pltpu.make_async_copy(sum_ref.at[:, part], out_ref.at[:, part], sems.at[g])
            )
    for copy in copies:
        copy.start()
    for g in range(groups):
        b = (g + 1) * share - 1
        if b < bands:

            def one(d, carry):
                for x in range(wide):
                    last_ref[g, d, x] = sum_ref[d, b, x] + home_back[d, b, x]
                return carry

            lax.fori_loop(0, local_dirs, one, 0, unroll=8)
            copy = pltpu.make_async_copy(last_ref.at[g], out_ref.at[:, b], sems.at[groups + g])
            copy.start()
            copies.append(copy)
    for copy in copies:
        copy.wait()


def both_ways(speed):
    centre, near, far = beam_coeffs(jnp.abs(speed))
    forward = speed > 0
    return (
        centre,
        jnp.where(forward, near, 0.0),
        jnp.where(forward, far, 0.0),
        jnp.where(forward, 0.0, near),
        jnp.where(forward, 0.0, far),
    )


def combine(coef, moves):
    total = coef[0] * moves[0]
    for c, move in zip(coef[1:], moves[1:]):
        total = total + c * move
    return total


def steps(tiles, groups, share, scalars, walls, vectors, home):
    local_dirs, _, wide, high, deep = home.shape
    dirs, rows = local_dirs * groups, wide * high
    part = dirs // tiles
    bands = scalars[2].shape[0]
    halves = 2 if groups % 2 == 0 and deep % (2 * BLOCK) == 0 else 1
    half = deep // halves
    vmem = pl.BlockSpec(memory_space=pltpu.VMEM)
    anywhere = pl.BlockSpec(memory_space=pl.ANY)
    dma = pltpu.SemaphoreType.DMA
    scratch = (
        [pltpu.VMEM((dirs, wide, high, deep), jnp.float32)] * share
        + [pltpu.VMEM((dirs, rows, deep), jnp.float32)] * share
        + [pltpu.VMEM((tiles, part, rows, deep), jnp.float32)] * (2 * share)
        + [pltpu.VMEM((dirs, rows, deep), jnp.float32)] * share
        + [pltpu.VMEM((dirs, wide, high, deep), jnp.float32)] * share
        + [
            pltpu.SMEM((1, dirs), jnp.int32),
            pltpu.SMEM((1, dirs), jnp.int32),
            pltpu.VMEM((2, 1, dirs), jnp.int32),
            pltpu.VMEM((rows, deep), jnp.float32),
            pltpu.SMEM((bands * local_dirs * (12 + len(set(n % high for n in WAYS) - {0})),), jnp.float32),
            pltpu.VMEM((tiles, OCT, rows, deep), jnp.float32),
            pltpu.VMEM((tiles, rows, deep), jnp.float32),
            pltpu.VMEM((2, tiles, rows, deep), jnp.float32),
            pltpu.VMEM((tiles, 2, rows, deep), jnp.float32),
            pltpu.VMEM((2, halves, rows, half), jnp.float32),
            pltpu.VMEM((2, rows, half), jnp.float32),
            pltpu.VMEM((2, rows, half), jnp.float32),
            pltpu.VMEM((2, groups // halves, rows, half), jnp.float32),
            pltpu.VMEM((halves, rows, half), jnp.float32),
            pltpu.VMEM((rows, half), jnp.float32),
            pltpu.VMEM((rows, half), jnp.float32),
            pltpu.VMEM((tiles, halves, rows, half), jnp.float32),
            dma((share, groups)),
            dma((share, groups)),
            dma((share, tiles)),
            dma((share, tiles)),
            dma((share, tiles)),
            dma((share, tiles)),
            dma((share, groups)),
            dma((share, groups)),
            dma((tiles,)),
            dma((tiles,)),
            dma((2, tiles)),
            dma((2, tiles)),
            dma((3,)),
            dma((3,)),
            dma((2, groups)),
            dma((2, groups)),
            dma((halves * tiles,)),
            dma((halves * tiles,)),
            dma((7, share)),
        ]
    )
    held = [pltpu.SMEM(v.shape, v.dtype) for v in (*scalars, *walls[:2])]
    held += [pltpu.VMEM(v.shape, v.dtype) for v in (*vectors, walls[2])]
    parts = pl.pallas_call(
        functools.partial(steps_kernel, tiles, groups, len(held)),
        in_specs=[anywhere] * (len(held) + 1),
        out_specs=[vmem] * 3,
        out_shape=[
            pltpu.VMEM((local_dirs, bands, wide, high, deep), jnp.float32),
            pltpu.VMEM((local_dirs, share * groups, wide, high, deep), jnp.float32),
            pltpu.VMEM((wide, high, deep), jnp.float32),
        ],
        scratch_shapes=held + scratch + [dma((len(held),))],
        compiler_params=pltpu.CompilerParams(
            collective_id=0, has_side_effects=True, vmem_limit_bytes=46 << 20
        ),
    )(*scalars, *walls[:2], *vectors, walls[2], home)
    return pl.pallas_call(
        functools.partial(settle_kernel, groups),
        in_specs=[vmem] * 3,
        out_specs=[anywhere] * 2,
        out_shape=[
            jax.ShapeDtypeStruct((local_dirs, bands, wide, high, deep), jnp.float32),
            jax.ShapeDtypeStruct((wide, high, deep), jnp.float32),
        ],
        scratch_shapes=[
            pltpu.VMEM((groups, local_dirs, wide, high, deep), jnp.float32),
            dma((2 * groups + 1,)),
        ],
        compiler_params=pltpu.CompilerParams(vmem_limit_bytes=4 << 20),
    )(*parts)


def beam_coeffs(abs_speed):
    return (
        1.0 - 1.5 * abs_speed + 0.5 * abs_speed * abs_speed,
        2.0 * abs_speed - abs_speed * abs_speed,
        0.5 * abs_speed * abs_speed - 0.5 * abs_speed,
    )


def on_device(
    phonon_heat_density,
    directions,
    quad_weight,
    mirror,
    band_courant,
    relax_rate,
    mode_heat_magnitude,
    mode_pulsation,
    wall_blocks,
    wall_count,
    wall_facet,
):
    local_dirs, bands, wide, high, deep = phonon_heat_density.shape
    tiles, groups = lax.axis_size("space"), lax.axis_size("dir")
    share = -(-bands // groups)
    extra = share * groups - bands
    home = phonon_heat_density
    if extra:
        home = jnp.pad(home, ((0, 0), (0, extra), (0, 0), (0, 0), (0, 0)))
    scalars = (
        directions,
        quad_weight,
        band_courant,
        relax_rate,
        mode_heat_magnitude,
        mode_pulsation,
    )
    walls = (wall_blocks, wall_count, wall_facet)
    return steps(tiles, groups, share, scalars, walls, (directions, mirror), home)


def solution(mesh):
    in_specs = (
        P("dir", None, "space", None, None),
        P(),
        P(),
        P(),
        P(),
        P(),
        P(),
        P(),
        P("space", None),
        P("space"),
        P("space", None, None),
    )
    out_specs = (P("dir", None, "space", None, None), P("space", None, None))
    return jax.shard_map(
        on_device, mesh=mesh, in_specs=in_specs, out_specs=out_specs, check_vma=False
    )
```

```python
import functools

import jax
import jax.numpy as jnp
from jax import lax
from jax.experimental import pallas as pl
from jax.experimental.pallas import tpu as pltpu
from jax.sharding import PartitionSpec as P

NEWTON = 4
BLOCK = 128
OCT = 8


def flat(values, axis):
    return jnp.sum(values, axis=axis, keepdims=True)


def orbit_order(directions, mirror):
    count = directions.shape[1]
    lane = lax.broadcasted_iota(jnp.int32, (count, count), 1).astype(jnp.float32)
    line = lax.broadcasted_iota(jnp.int32, (count, count), 0).astype(jnp.float32)
    same = lane == line
    positive = [jnp.where(directions[a : a + 1] > 0, 1.0, 0.0) for a in range(3)]
    code = positive[0] + 2.0 * positive[1] + 4.0 * positive[2]
    rep = flat(jnp.where(same, lane, 0.0), 1)
    for a in range(3):
        partner = mirror[a : a + 1].astype(jnp.float32)
        flipped = flat(jnp.where(rep == lane, partner, 0.0), 1)
        ahead = flat(jnp.where(same, positive[a], 0.0), 1)
        rep = jnp.where(ahead > 0.5, rep, flipped)
    rank = flat(jnp.where(lane < rep, jnp.where(code == OCT - 1, 1.0, 0.0), 0.0), 1)
    position = OCT * rank + flat(jnp.where(same, code, 0.0), 1)
    order = flat(jnp.where(position == lane, line, 0.0), 0)
    position = flat(jnp.where(same, position, 0.0), 0)
    return [jnp.clip(v.astype(jnp.int32), 0, count - 1) for v in (order, position)]


def facet_grid(blocks_ref, count_ref, wall_ref, rows, deep):
    cuts = deep // BLOCK
    row_id = lax.broadcasted_iota(jnp.int32, (rows, BLOCK), 0)
    grid = []
    for h in range(cuts):
        facets = jnp.zeros((rows, BLOCK), jnp.int32)
        for slot in range(wall_ref.shape[1]):
            block = jnp.where(slot < count_ref[0], blocks_ref[0, slot], -1)
            facets = jnp.where(
                row_id * cuts + h == block, wall_ref[0, slot : slot + 1, :], facets
            )
        grid.append(facets.astype(jnp.float32))
    return grid


def roll(u, by, axis):
    return pltpu.roll(u, by % u.shape[axis], axis)


def unit_coeffs(scalars, band, orbit):
    order_ref, directions_ref, weight_ref, courant_ref, rate_ref = scalars
    bands = courant_ref.shape[0]
    real = band < bands
    index = jnp.minimum(band, bands - 1)
    courant, rate = courant_ref[index], jnp.where(real, rate_ref[index], 0.0)
    rep = order_ref[0, orbit * OCT + OCT - 1]
    coef = []
    for axis_num in range(3):
        coef.extend(beam_coeffs(courant * jnp.abs(directions_ref[axis_num, rep])))
    coef.append(rate * weight_ref[rep])
    return coef, rate


def surplus_of(q):
    series = jnp.ones_like(q)
    for n in range(9, 1, -1):
        series = 1.0 + series * (q * (1.0 / n))
    return jnp.where(q < 0.5, q * series, jnp.exp(q) - 1.0)


def newton(rate_ref, magnitude_ref, pulsation_ref, source):
    kelvin = jnp.ones_like(source)
    for newton_turn in range(NEWTON):
        inverse = 1.0 / kelvin

        def one(b, carry):
            mismatch, gradient = carry
            factor = rate_ref[b] * magnitude_ref[b]
            q = pulsation_ref[b] * inverse
            surplus = surplus_of(q)
            ratio = 1.0 / surplus
            term = factor * ratio
            return mismatch + term, gradient + term * q * ((surplus + 1.0) * ratio)

        zero = jnp.zeros_like(source)
        mismatch, gradient = lax.fori_loop(0, rate_ref.shape[0], one, (zero, zero), unroll=8)
        mismatch, gradient = mismatch - source, gradient * inverse
        kelvin = jnp.clip(kelvin - mismatch / gradient, 0.5 * kelvin, 2.0 * kelvin)
    return kelvin


def sweep_unit(high, tiles, coef, facets_ref, load, store):
    _, rows, width = facets_ref.shape
    row_id = lax.broadcasted_iota(jnp.int32, (rows, width), 0)
    height = row_id % high
    total = [jnp.zeros((rows, width), jnp.float32) for _ in range(tiles)]
    for o in range(OCT):
        way = [1 if o >> a & 1 else -1 for a in range(3)]
        cells = []
        for t in range(tiles):
            facets = facets_ref[t]
            u = load(t, o)
            for a in range(3):
                facing = float(2 * a + 1 if way[a] > 0 else 2 * a + 2)
                u = jnp.where(facets == facing, load(t, o ^ (1 << a)), u)
            cells.append(u)
        turned = [roll(u, high * way[0], 0) for u in cells]
        for t in range(tiles):
            up = (t - way[0]) % tiles
            edge = row_id < high if way[0] > 0 else row_id >= rows - high
            near = jnp.where(edge, turned[up], turned[t])
            u = coef[0] * cells[t] + coef[1] * near + coef[2] * cells[up]
            u = coef[3] * u + coef[4] * roll(u, way[1], 1) + coef[5] * roll(u, 2 * way[1], 1)
            wrap1 = height < 1 if way[2] > 0 else height >= high - 1
            wrap2 = height < 2 if way[2] > 0 else height >= high - 2
            near = jnp.where(wrap1, roll(u, (1 - high) * way[2], 0), roll(u, way[2], 0))
            far = jnp.where(wrap2, roll(u, (2 - high) * way[2], 0), roll(u, 2 * way[2], 0))
            u = coef[6] * u + coef[7] * near + coef[8] * far
            store(t, o, u)
            total[t] = total[t] + u
    return [coef[9] * total[t] for t in range(tiles)]


MESH = pl.DeviceIdType.MESH


def greet(tile, tiles, group, groups, halves):
    barrier = pltpu.get_barrier_semaphore()
    peers = [(lax.rem(tile + u, tiles), group) for u in range(1, tiles)]
    peers += [(tile, lax.rem(group + t, groups)) for t in range(1, groups)]
    if halves > 1:
        peers += [(lax.rem(tile + u, tiles), lax.bitwise_xor(group, 1)) for u in range(1, tiles)]
    for peer in reversed(peers):
        pl.semaphore_signal(barrier, inc=1, device_id=peer, device_id_type=MESH)
    return barrier, len(peers)


def remote(src, dst, send, recv, device):
    return pltpu.make_async_remote_copy(
        src_ref=src, dst_ref=dst, send_sem=send, recv_sem=recv, device_id=device, device_id_type=MESH
    )


WAYS = (1, 2, -1, -2)
UNROLL = 8


def steps_kernel(
    tiles, groups, small, *refs
):
    given, (home_ref, out_ref, home_back, kelvin_ref) = refs[:small], refs[small : small + 4]
    held, scratch = refs[small + 4 : 2 * small + 4], refs[2 * small + 4 : -1]
    (
        directions_ref, weight_ref, courant_ref, rate_ref, magnitude_ref, pulsation_ref, blocks_ref,
        count_ref, vectors_ref, mirror_ref, wall_ref,
    ) = held
    inputs = [
        pltpu.make_async_copy(src, dst, refs[-1].at[n])
        for n, (src, dst) in enumerate(zip(given, held))
    ]
    local_dirs, slots, wide, high, deep = home_ref.shape
    share, rows, bands = slots // groups, wide * high, courant_ref.shape[0]
    dirs = local_dirs * groups
    part = dirs // tiles
    orbits = part // OCT
    landed, sorted_refs, fields, swept, back, unsorted = (
        scratch[n * share : (n + 1) * share] for n in range(6)
    )
    (
        order_ref, position_ref, ids_ref, facet_ref, coef_ref, between, facets_ref, source_ref, near, summed, near_half,
        partial_ref, far, found, given_half, shared, kelvins,
        dir_send, dir_recv, tile_send, tile_recv, rev_send, rev_recv, ret_send, ret_recv,
        facet_send, facet_recv, near_send, near_recv, pair_send, pair_recv, far_send, far_recv, last_send, last_recv, own_sem,
    ) = scratch[6 * share :]
    scalars = (order_ref, directions_ref, weight_ref, courant_ref, rate_ref)
    tile, group = lax.axis_index("space"), lax.axis_index("dir")

    halves = summed.shape[1]
    half = deep // halves
    mine = lax.rem(group, halves)
    mate = (tile, lax.bitwise_xor(group, 1))
    lanes = [slice(h * half, (h + 1) * half) for h in range(halves)]

    def to_tiles(u):
        return (lax.rem(tile + u, tiles), group)

    def other(t):
        if groups & (groups - 1):
            return lax.rem(group + t, groups)
        return lax.bitwise_xor(group, t)

    visits = list(range(1, groups))
    if groups % 2 == 0:
        visits = [t ^ 1 for t in visits[1:3]] + visits[:1] + [t ^ 1 for t in visits[3:]]

    def sender(t):
        if groups & (groups - 1):
            return lax.rem(group + groups - t, groups)
        return lax.bitwise_xor(group, t)

    def to_groups(t):
        return (tile, other(t))

    own = [
        pltpu.make_async_copy(
            home_ref.at[:, group * share + k],
            landed[k].at[pl.ds(group * local_dirs, local_dirs)],
            own_sem.at[0, k],
        )
        for k in range(share)
    ]
    barrier, greeted = greet(tile, tiles, group, groups, halves)
    for copy in own + inputs:
        copy.start()
    pl.semaphore_wait(barrier, greeted)

    first = []
    for k in range(share):
        line = []
        for t in visits:
            peer = other(t)
            copy = remote(
                home_ref.at[:, peer * share + k],
                landed[k].at[pl.ds(group * local_dirs, local_dirs)],
                dir_send.at[k, t],
                dir_recv.at[k, t],
                to_groups(t),
            )
            copy.start()
            line.append(copy)
        first.append(line)

    for copy in inputs:
        copy.wait()
    order, position = orbit_order(vectors_ref[...], mirror_ref[...])
    ids_ref[0] = order
    ids_ref[1] = position
    tables = [
        pltpu.make_async_copy(ids_ref.at[0], order_ref, own_sem.at[5, 0]),
        pltpu.make_async_copy(ids_ref.at[1], position_ref, own_sem.at[6, 0]),
    ]
    for copy in tables:
        copy.start()
    for h, facets in enumerate(facet_grid(blocks_ref, count_ref, wall_ref, rows, deep)):
        facet_ref[:, h * BLOCK : (h + 1) * BLOCK] = facets
    own_facets = pltpu.make_async_copy(facet_ref, facets_ref.at[tile], own_sem.at[4, 0])
    own_facets.start()
    third = []
    for u in range(1, tiles):
        copy = remote(
            facet_ref, facets_ref.at[tile], facet_send.at[u], facet_recv.at[u], to_tiles(u)
        )
        copy.start()
        third.append(copy)
    source_ref[...] = jnp.zeros_like(source_ref)

    second, fourth, fifth = [], [], []
    turns = sorted(set(n % high for n in WAYS) - {0})
    width = 12 + len(turns)

    def table(b, carry):
        def one(d, carry):
            index, base = group * local_dirs + d, (b * local_dirs + d) * width
            line = []
            for a in range(3):
                line.append(both_ways(courant_ref[b] * directions_ref[a, index]))
            cz = [line[2][0]] + [0.0] * len(turns)
            for n, c in zip(WAYS, line[2][1:]):
                at = turns.index(n % high) + 1 if n % high else 0
                cz[at] = cz[at] + c
            values = list(line[0]) + list(line[1]) + cz
            values.append(rate_ref[b] * rate_ref[b] * weight_ref[index])
            for n, value in enumerate(values):
                coef_ref[base + n] = value
            return carry

        return lax.fori_loop(0, local_dirs, one, carry)

    lax.fori_loop(0, bands, table, 0)
    for copy in tables:
        copy.wait()

    last, early = share - 1, max(share - 3, 0)

    def gather(k):
        own[k].wait()
        for copy in first[k]:
            copy.wait_recv()

        def move(j, carry):
            d = order_ref[0, j]
            for x in range(wide):
                sorted_refs[k][j, x * high : (x + 1) * high, :] = landed[k][d, x]
            return carry

        lax.fori_loop(0, dirs, move, 0, unroll=16)
        line = [
            pltpu.make_async_copy(
                sorted_refs[k].at[pl.ds(tile * part, part)], fields[k].at[tile], own_sem.at[1, k]
            )
        ]
        for u in range(1, tiles):
            peer = lax.rem(tile + u, tiles)
            line.append(
                remote(
                    sorted_refs[k].at[pl.ds(peer * part, part)],
                    fields[k].at[tile],
                    tile_send.at[k, u],
                    tile_recv.at[k, u],
                    to_tiles(u),
                )
            )
        for copy in line:
            copy.start()
        second.append(line)

    def first_half(k, orbit, keep):
        coef, _ = unit_coeffs(scalars, group * share + k, tile * orbits + orbit)
        sums = sweep_unit(
            high, tiles, coef, facets_ref, lambda t, o: fields[k][t, orbit * OCT + o], keep
        )
        for t in range(tiles):
            source_ref[0, t] = source_ref[0, t] + sums[t]

    def second_half(k, orbit, load, result):
        coef, rate = unit_coeffs(scalars, group * share + k, tile * orbits + orbit)
        left = 1.0 - rate
        coef = coef[:6] + [left * c for c in coef[6:9]] + coef[9:]

        def keep(t, o, u):
            result[t, orbit * OCT + o] = left * u

        sums = sweep_unit(high, tiles, coef, facets_ref, load, keep)
        for t in range(tiles):
            source_ref[1, t] = source_ref[1, t] + sums[t]

    def arrive(k):
        second[k][0].wait()
        for copy in second[k][1:]:
            copy.wait_recv()

    def sweep(k):
        arrive(k)

        def one(orbit, carry):
            def keep(t, o, u):
                between[t, o] = u

            first_half(k, orbit, keep)
            second_half(k, orbit, lambda t, o: between[t, o], swept[k])
            return carry

        lax.fori_loop(0, orbits, one, 0)

    def sweep_first(k):
        arrive(k)

        def one(orbit, carry):
            def keep(t, o, u):
                swept[k][t, orbit * OCT + o] = u

            first_half(k, orbit, keep)
            return carry

        lax.fori_loop(0, orbits, one, 0)

    def sweep_second(k):
        def one(orbit, carry):
            second_half(k, orbit, lambda t, o: swept[k][t, orbit * OCT + o], fields[k])
            return carry

        lax.fori_loop(0, orbits, one, 0)

    def turn(k):
        done = fields[k] if k == last else swept[k]
        line = [
            pltpu.make_async_copy(
                done.at[tile], back[k].at[pl.ds(tile * part, part)], own_sem.at[2, k]
            )
        ]
        for u in range(1, tiles):
            peer = lax.rem(tile + u, tiles)
            line.append(
                remote(
                    done.at[peer],
                    back[k].at[pl.ds(tile * part, part)],
                    rev_send.at[k, u],
                    rev_recv.at[k, u],
                    to_tiles(u),
                )
            )
        for copy in line:
            copy.start()
        fourth.append(line)

    def scatter(k):
        fourth[k][0].wait()
        for copy in fourth[k][1:]:
            copy.wait_recv()

        def move(d, carry):
            j = position_ref[0, d]
            for x in range(wide):
                unsorted[k][d, x] = back[k][j, x * high : (x + 1) * high, :]
            return carry

        lax.fori_loop(0, dirs, move, 0, unroll=16)

    def send_home(k):
        line = [
            pltpu.make_async_copy(
                unsorted[k].at[pl.ds(group * local_dirs, local_dirs)],
                home_back.at[:, group * share + k],
                own_sem.at[3, k],
            )
        ]
        for t in visits:
            peer = other(t)
            line.append(
                remote(
                    unsorted[k].at[pl.ds(peer * local_dirs, local_dirs)],
                    home_back.at[:, group * share + k],
                    ret_send.at[k, t],
                    ret_recv.at[k, t],
                    to_groups(t),
                )
            )
        for copy in line:
            copy.start()
        fifth.append(line)

    def sum_groups(n):
        value, copies = summed[n, mine], []
        if halves > 1:
            copy = remote(
                summed.at[n, 1 - mine], near_half.at[n], pair_send.at[n], pair_recv.at[n], mate
            )
            copy.start()
            copy.wait_recv()
            value = value + near_half[n]
            copies.append(copy)
        partial_ref[n] = value
        place = group // halves
        fars = []
        for t in range(1, groups // halves):
            fars.append(
                remote(
                    partial_ref.at[n],
                    far.at[n, place],
                    far_send.at[n, t],
                    far_recv.at[n, t],
                    to_groups(t * halves),
                )
            )
        for copy in fars:
            copy.start()
        far[n, place] = value
        return copies, fars

    def total_of(n, copies):
        for copy in copies:
            copy.wait_recv()
        value = far[n, 0]
        for g in range(1, groups // halves):
            value = value + far[n, g]
        return newton(rate_ref, magnitude_ref, pulsation_ref, value)

    for k in range(share):
        if k > 0:
            sweep(k - 1)
            if k - 1 < early:
                turn(k - 1)
        gather(k)
        if k == 0:
            own_facets.wait()
            for copy in third:
                copy.wait_recv()
        if 2 <= k < early + 2:
            scatter(k - 2)
            send_home(k - 2)
    def sum_tiles(n):
        copies = []
        for u in range(1, tiles):
            peer = lax.rem(tile + u, tiles)
            copy = remote(
                source_ref.at[n, peer],
                near.at[u, n],
                near_send.at[n, u],
                near_recv.at[n, u],
                to_tiles(u),
            )
            copy.start()
            copies.append(copy)
        return copies

    def sum_of(n, copies):
        value = source_ref[n, tile]
        for u in range(1, tiles):
            copies[u - 1].wait_recv()
            value = value + near[u, n]
        return value

    sweep_first(last)
    nears = sum_tiles(0)
    for k in range(early, last):
        turn(k)
    sweep_second(last)
    value = sum_of(0, nears)
    for h in range(halves):
        summed[0, h] = value[:, lanes[h]]
    pairs, fars = sum_groups(0)
    while len(fifth) < share - 1:
        scatter(len(fifth))
        send_home(len(fifth))
    value = total_of(0, fars)
    shared[...] = value
    lasts = []
    for u in range(tiles):
        for m in range(halves):
            if u or m:
                target = (lax.rem(tile + u, tiles), lax.bitwise_xor(group, m))
                n = u * halves + m
                copy = remote(
                    shared, kelvins.at[tile, mine], last_send.at[n], last_recv.at[n], target
                )
                copy.start()
                lasts.append(copy)
    kelvins[tile, mine] = value
    last_nears = sum_tiles(1)
    turn(last)
    for copy in lasts:
        copy.wait_recv()

    below, above = lax.rem(tile + tiles - 1, tiles), lax.rem(tile + 1, tiles)
    row_id = lax.broadcasted_iota(jnp.int32, (rows, deep), 0)
    height = row_id % high

    def spin(u, n):
        return jnp.where(height < n, roll(u, n - high, 0), roll(u, n, 0))

    def drift_coeffs(d, b):
        base = (b * local_dirs + d) * width
        values = [coef_ref[base + n] for n in range(width)]
        return values[:5], values[5:10], values[10:-1], values[-1]

    def drift(b, acc):
        left = (1.0 - rate_ref[b]) * rate_ref[b]

        def bose(t):
            warm = jnp.concatenate([kelvins[t, h] for h in range(halves)], axis=1)
            return magnitude_ref[b] / surplus_of(pulsation_ref[b] / warm)

        here, low, up = bose(tile), bose(below), bose(above)
        shifted = [
            here,
            jnp.where(row_id < high, roll(low, high, 0), roll(here, high, 0)),
            low,
            jnp.where(row_id >= rows - high, roll(up, -high, 0), roll(here, -high, 0)),
            up,
        ]

        def one(d, acc):
            cx, cy, cz, weight = drift_coeffs(d, b)
            u = combine(cx, shifted)
            u = combine(cy, [u] + [roll(u, n, 1) for n in WAYS])
            u = combine(cz, [u] + [spin(u, n) for n in turns])
            kept = left * u
            for x in range(wide):
                out_ref[d, b, x] = kept[x * high : (x + 1) * high]
            return acc + weight * u

        return lax.fori_loop(0, local_dirs, one, acc, unroll=UNROLL)

    acc = lax.fori_loop(0, bands, drift, jnp.zeros((rows, deep), jnp.float32))
    value = sum_of(1, last_nears) + acc
    for h in range(halves):
        summed[1, h] = value[:, lanes[h]]
    pair, last_fars = sum_groups(1)
    scatter(last)
    send_home(last)
    value = total_of(1, last_fars)
    found[mine] = value
    if halves > 1:
        given_half[...] = value
        copy = remote(given_half, found.at[mine], pair_send.at[2], pair_recv.at[2], mate)
        copy.start()
        copy.wait_recv()
        pair.append(copy)
    for h in range(halves):
        value = found[h]
        for x in range(wide):
            kelvin_ref[x, :, lanes[h]] = value[x * high : (x + 1) * high]
    fars = pairs + fars + pair + last_fars + last_nears

    def settle(b, carry):
        warm = jnp.concatenate([found[h] for h in range(halves)], axis=1)
        heat = rate_ref[b] * (magnitude_ref[b] / surplus_of(pulsation_ref[b] / warm))

        def one(d, carry):
            for x in range(wide):
                out_ref[d, b, x] = out_ref[d, b, x] + heat[x * high : (x + 1) * high]
            return carry

        return lax.fori_loop(0, local_dirs, one, carry, unroll=4)

    lax.fori_loop(0, bands, settle, 0)
    for k in range(share):
        for n, t in enumerate([0] + visits):
            if n:
                fifth[k][n].wait_recv()
            else:
                fifth[k][0].wait()
            if k == last:
                continue
            b = sender(t) * share + k

            def one(d, carry):
                for x in range(wide):
                    out_ref[d, b, x] = out_ref[d, b, x] + home_back[d, b, x]
                return carry

            if share * groups == bands:
                lax.fori_loop(0, local_dirs, one, 0, unroll=8)
            else:
                lax.fori_loop(0, jnp.where(b < bands, local_dirs, 0), one, 0)
    for copy in third + nears + fars + lasts:
        copy.wait_send()
    for line in first:
        for copy in line:
            copy.wait_send()
    for line in second + fourth + fifth:
        for copy in line[1:]:
            copy.wait_send()


def settle_kernel(groups, sum_ref, home_back, kelvin_ref, out_ref, kelvin_out, last_ref, sems):
    local_dirs, bands, wide = sum_ref.shape[:3]
    share = home_back.shape[1] // groups
    copies = [pltpu.make_async_copy(kelvin_ref, kelvin_out, sems.at[2 * groups])]
    for g in range(groups):
        count = min(bands - g * share, share - 1)
        if count > 0:
            part = pl.ds(g * share, count)
            copies.append(
                pltpu.make_async_copy(sum_ref.at[:, part], out_ref.at[:, part], sems.at[g])
            )
    for copy in copies:
        copy.start()
    for g in range(groups):
        b = (g + 1) * share - 1
        if b < bands:

            def one(d, carry):
                for x in range(wide):
                    last_ref[g, d, x] = sum_ref[d, b, x] + home_back[d, b, x]
                return carry

            lax.fori_loop(0, local_dirs, one, 0, unroll=8)
            copy = pltpu.make_async_copy(last_ref.at[g], out_ref.at[:, b], sems.at[groups + g])
            copy.start()
            copies.append(copy)
    for copy in copies:
        copy.wait()


def both_ways(speed):
    centre, near, far = beam_coeffs(jnp.abs(speed))
    forward = speed > 0
    return (
        centre,
        jnp.where(forward, near, 0.0),
        jnp.where(forward, far, 0.0),
        jnp.where(forward, 0.0, near),
        jnp.where(forward, 0.0, far),
    )


def combine(coef, moves):
    total = coef[0] * moves[0]
    for c, move in zip(coef[1:], moves[1:]):
        total = total + c * move
    return total


def steps(tiles, groups, share, scalars, walls, vectors, home):
    local_dirs, _, wide, high, deep = home.shape
    dirs, rows = local_dirs * groups, wide * high
    part = dirs // tiles
    bands = scalars[2].shape[0]
    halves = 2 if groups % 2 == 0 and deep % (2 * BLOCK) == 0 else 1
    half = deep // halves
    vmem = pl.BlockSpec(memory_space=pltpu.VMEM)
    anywhere = pl.BlockSpec(memory_space=pl.ANY)
    dma = pltpu.SemaphoreType.DMA
    scratch = (
        [pltpu.VMEM((dirs, wide, high, deep), jnp.float32)] * share
        + [pltpu.VMEM((dirs, rows, deep), jnp.float32)] * share
        + [pltpu.VMEM((tiles, part, rows, deep), jnp.float32)] * (2 * share)
        + [pltpu.VMEM((dirs, rows, deep), jnp.float32)] * share
        + [pltpu.VMEM((dirs, wide, high, deep), jnp.float32)] * share
        + [
            pltpu.SMEM((1, dirs), jnp.int32),
            pltpu.SMEM((1, dirs), jnp.int32),
            pltpu.VMEM((2, 1, dirs), jnp.int32),
            pltpu.VMEM((rows, deep), jnp.float32),
            pltpu.SMEM((bands * local_dirs * (12 + len(set(n % high for n in WAYS) - {0})),), jnp.float32),
            pltpu.VMEM((tiles, OCT, rows, deep), jnp.float32),
            pltpu.VMEM((tiles, rows, deep), jnp.float32),
            pltpu.VMEM((2, tiles, rows, deep), jnp.float32),
            pltpu.VMEM((tiles, 2, rows, deep), jnp.float32),
            pltpu.VMEM((2, halves, rows, half), jnp.float32),
            pltpu.VMEM((2, rows, half), jnp.float32),
            pltpu.VMEM((2, rows, half), jnp.float32),
            pltpu.VMEM((2, groups // halves, rows, half), jnp.float32),
            pltpu.VMEM((halves, rows, half), jnp.float32),
            pltpu.VMEM((rows, half), jnp.float32),
            pltpu.VMEM((rows, half), jnp.float32),
            pltpu.VMEM((tiles, halves, rows, half), jnp.float32),
            dma((share, groups)),
            dma((share, groups)),
            dma((share, tiles)),
            dma((share, tiles)),
            dma((share, tiles)),
            dma((share, tiles)),
            dma((share, groups)),
            dma((share, groups)),
            dma((tiles,)),
            dma((tiles,)),
            dma((2, tiles)),
            dma((2, tiles)),
            dma((3,)),
            dma((3,)),
            dma((2, groups)),
            dma((2, groups)),
            dma((halves * tiles,)),
            dma((halves * tiles,)),
            dma((7, share)),
        ]
    )
    held = [pltpu.SMEM(v.shape, v.dtype) for v in (*scalars, *walls[:2])]
    held += [pltpu.VMEM(v.shape, v.dtype) for v in (*vectors, walls[2])]
    parts = pl.pallas_call(
        functools.partial(steps_kernel, tiles, groups, len(held)),
        in_specs=[pl.BlockSpec(memory_space=pltpu.HBM)] * (len(held) + 1),
        out_specs=[vmem] * 3,
        out_shape=[
            pltpu.VMEM((local_dirs, bands, wide, high, deep), jnp.float32),
            pltpu.VMEM((local_dirs, share * groups, wide, high, deep), jnp.float32),
            pltpu.VMEM((wide, high, deep), jnp.float32),
        ],
        scratch_shapes=held + scratch + [dma((len(held),))],
        compiler_params=pltpu.CompilerParams(
            collective_id=0, has_side_effects=True, vmem_limit_bytes=46 << 20
        ),
    )(*scalars, *walls[:2], *vectors, walls[2], home)
    return pl.pallas_call(
        functools.partial(settle_kernel, groups),
        in_specs=[vmem] * 3,
        out_specs=[anywhere] * 2,
        out_shape=[
            jax.ShapeDtypeStruct((local_dirs, bands, wide, high, deep), jnp.float32),
            jax.ShapeDtypeStruct((wide, high, deep), jnp.float32),
        ],
        scratch_shapes=[
            pltpu.VMEM((groups, local_dirs, wide, high, deep), jnp.float32),
            dma((2 * groups + 1,)),
        ],
        compiler_params=pltpu.CompilerParams(vmem_limit_bytes=4 << 20),
    )(*parts)


def beam_coeffs(abs_speed):
    return (
        1.0 - 1.5 * abs_speed + 0.5 * abs_speed * abs_speed,
        2.0 * abs_speed - abs_speed * abs_speed,
        0.5 * abs_speed * abs_speed - 0.5 * abs_speed,
    )


def on_device(
    phonon_heat_density,
    directions,
    quad_weight,
    mirror,
    band_courant,
    relax_rate,
    mode_heat_magnitude,
    mode_pulsation,
    wall_blocks,
    wall_count,
    wall_facet,
):
    local_dirs, bands, wide, high, deep = phonon_heat_density.shape
    tiles, groups = lax.axis_size("space"), lax.axis_size("dir")
    share = -(-bands // groups)
    extra = share * groups - bands
    home = phonon_heat_density
    if extra:
        home = jnp.pad(home, ((0, 0), (0, extra), (0, 0), (0, 0), (0, 0)))
    scalars = (
        directions,
        quad_weight,
        band_courant,
        relax_rate,
        mode_heat_magnitude,
        mode_pulsation,
    )
    walls = (wall_blocks, wall_count, wall_facet)
    return steps(tiles, groups, share, scalars, walls, (directions, mirror), home)


def solution(mesh):
    in_specs = (
        P("dir", None, "space", None, None),
        P(),
        P(),
        P(),
        P(),
        P(),
        P(),
        P(),
        P("space", None),
        P("space"),
        P("space", None, None),
    )
    out_specs = (P("dir", None, "space", None, None), P("space", None, None))
    return jax.shard_map(
        on_device, mesh=mesh, in_specs=in_specs, out_specs=out_specs, check_vma=False
    )
```
